512 devices in a mesh: section: 8 (over y, z_hi), dp: 16 (over z_lo, core), chan: 4 (over x).
Axes of the slice: x: 4, y: 4, z: 16 (z_hi: 2, z_lo: 8; z = z_hi * 8 + z_lo), core: 2. Of those that a mesh axis runs over, the one named last changes fastest.
Arguments:
- clips: bfloat16 [2, 512, 2048], P(None, 'chan', 'dp'), may hold values from -6 to 6
- weights: bfloat16 [8, 512, 27, 512], P('section', ('chan', 'dp')), may hold values from -0.0546875 to 0.0546875
- cotangents: bfloat16 [2, 512, 2048], P(None, 'chan', 'dp'), may hold values from -0.5 to 0.5
Outputs:
- weight_grads: float32 [8, 512, 27, 512], P('section', ('chan', 'dp'))
The draws below stay inside these ranges and needn't reach their ends.
All inputs are finite; a program needn't handle non-finite values.
Results may differ from the reference program's by a relative error of at most 0.019.
Values may be sent and summed in bfloat16 or wider, within the bound.
No kernel may reach another device: no remote copies, remote signals or barrier semaphores. Data moves between devices by JAX's collectives and lax.ppermute only.
A program may use at most 128 MiB of HBM per device.

```python
import jax
import jax.numpy as jnp
from jax import lax

C = 512
FRAMES = 4
HEIGHT = 4
WIDTH = 8
MICRO = 2
DP_CELLS = 2048
LAYERS = 8


def with_spikes(values, rng, source, target, parts, factor):
    owner, partner = [(jnp.arange(values.shape[axis_at]) // (values.shape[axis_at] // parts)).reshape([-1 if axis == axis_at else 1 for axis in range(values.ndim)]) for axis_at in (source, target)]
    chosen = jax.random.permutation(rng, parts)[partner]
    strong = (owner == chosen) | (owner == (partner + parts // 2) % parts)
    return jnp.where(strong, factor * values, values)


def shard_levels(key, shape, shards, least, largest):
    gain, own = 1.0, jax.random.fold_in(key, 6)
    for dim, blocks in shards:
        draws = jnp.exp(jax.random.uniform(jax.random.fold_in(own, dim), (blocks,), jnp.float32, least / len(shards), largest / len(shards)))
        gain = gain * jnp.repeat(draws, shape[dim] // blocks).reshape([-1 if axis == dim else 1 for axis in range(len(shape))])
    return gain


def noise(own_key, shape, width, reach, cuts=(), kind=jnp.bfloat16):
    gain = shard_levels(own_key, shape, cuts, -0.22, 0.18) if cuts else 1.0
    drawn = jax.random.normal(own_key, shape, jnp.float32) * width * gain
    return jnp.minimum(jnp.maximum(drawn, -reach), reach).astype(kind)


def noise_with(stream_key, dims, width, limit, cuts, heavy, kind=jnp.bfloat16):
    array = width * jax.random.normal(stream_key, dims, jnp.float32)
    if cuts:
        array = array * shard_levels(stream_key, dims, cuts, -0.22, 0.18)
    return jnp.clip(with_spikes(array, jax.random.fold_in(stream_key, 3), *heavy), -limit, limit).astype(kind)


def setup_inputs(seed: int = 0) -> dict:
    arg_keys = jax.random.split(jax.random.key(seed), 4)
    clips = noise(arg_keys[0], (MICRO, C, DP_CELLS), 1.0, 6.0, ((1, 4), (2, 16)))
    weights = noise(arg_keys[1], (LAYERS, C, 27, C), (27 * C) ** -0.5, 0.0546875, ((0, 8), (1, 64)))
    cotangents = noise_with(arg_keys[2], (MICRO, C, DP_CELLS), (1.5 / (MICRO * DP_CELLS) ** 0.5), 0.5, ((1, 4), (2, 16)), (2, 1, 16, 2.0))
    return dict(clips=clips, weights=weights, cotangents=cotangents)


def silu_slope(values):
    sigmoid = jax.nn.sigmoid(values)
    return sigmoid * (1.0 + values * (1.0 - sigmoid))

def shifted_taps(source, time_shift, mirror, frames, height, columns):
    cell_count = source.shape[1]
    plane_size = height * columns
    margin = plane_size + columns + 1
    padded = jnp.pad(source, ((0, 0), (margin, margin)))
    position = jnp.arange(cell_count, dtype=jnp.int32)
    frame_of = position // plane_size % frames
    row_of = position // columns % height
    column_of = position % columns
    windows = []
    for row_shift in range(3):
        for column_shift in range(3):
            if mirror:
                move_frame, move_row, move_column = (1 - time_shift, 1 - row_shift, 1 - column_shift)
            else:
                move_frame, move_row, move_column = (time_shift - 1, row_shift - 1, column_shift - 1)
            offset = move_frame * plane_size + move_row * columns + move_column
            window = padded[:, margin + offset:margin + offset + cell_count]
            inside = (frame_of + move_frame >= 0) & (frame_of + move_frame < frames) & (row_of + move_row >= 0) & (row_of + move_row < height) & (column_of + move_column >= 0) & (column_of + move_column < columns)
            windows.append(jnp.where(inside[None, :], window, jnp.zeros_like(window)))
    return windows

def conv_forward(activated, kernel, frames, height, columns):
    outputs = kernel.shape[0]
    result = jnp.zeros((outputs, activated.shape[1]), jnp.float32)
    for time_shift in range(3):
        stacked = jnp.concatenate(shifted_taps(activated, time_shift, False, frames, height, columns), axis=0)
        matrix = kernel[:, 9 * time_shift:9 * time_shift + 9, :].reshape(outputs, -1)
        result = result + jnp.dot(matrix, stacked, preferred_element_type=jnp.float32)
    return result

def conv_weight_grad(activated, grad_low, frames, height, columns):
    pieces = []
    for time_shift in range(3):
        stacked = jnp.concatenate(shifted_taps(activated, time_shift, False, frames, height, columns), axis=0)
        product = lax.dot_general(grad_low, stacked, (((1,), (1,)), ((), ())), preferred_element_type=jnp.float32)
        pieces.append(product.reshape(grad_low.shape[0], 9, activated.shape[0]))
    return jnp.concatenate(pieces, axis=1)

def conv_input_grad(grads_all, kernel_back, frames, height, columns):
    inputs = kernel_back.shape[2]
    cell_count = grads_all.shape[1]
    result = jnp.zeros((inputs, cell_count), jnp.float32)
    for time_shift in range(3):
        stacked = jnp.stack(shifted_taps(grads_all, time_shift, True, frames, height, columns), axis=1)
        stacked = stacked.reshape(-1, cell_count)
        matrix = kernel_back[:, 9 * time_shift:9 * time_shift + 9, :].reshape(-1, inputs)
        result = result + lax.dot_general(matrix, stacked, (((0,), (0,)), ((), ())), preferred_element_type=jnp.float32)
    return result

def reference(clips, weights, cotangents):
    half_depth = LAYERS // 2
    weight_grads = [jnp.zeros(weights.shape[1:], jnp.float32) for layer_index in range(LAYERS)]
    for micro_index in range(MICRO):
        state_now = clips[micro_index]
        encoder_outputs = []
        saved = []
        for layer_index in range(LAYERS):
            summed = state_now.astype(jnp.float32)
            if layer_index >= half_depth:
                summed = summed + encoder_outputs[LAYERS - 1 - layer_index].astype(jnp.float32)
            activated = jax.nn.silu(summed).astype(jnp.bfloat16)
            update = conv_forward(activated, weights[layer_index], FRAMES, HEIGHT, WIDTH)
            state_now = lax.optimization_barrier((state_now.astype(jnp.float32) + update).astype(jnp.bfloat16))
            saved.append((summed, activated))
            if layer_index < half_depth:
                encoder_outputs.append(state_now)
        carried = cotangents[micro_index]
        skip_grads = {}
        for layer_index in reversed(range(LAYERS)):
            summed, activated = saved[layer_index]
            upstream = carried.astype(jnp.float32)
            if layer_index < half_depth:
                upstream = upstream + skip_grads[layer_index].astype(jnp.float32)
            grad_low = upstream.astype(jnp.bfloat16)
            weight_grads[layer_index] = weight_grads[layer_index] + conv_weight_grad(activated, grad_low, FRAMES, HEIGHT, WIDTH)
            pre_grad = conv_input_grad(grad_low, weights[layer_index], FRAMES, HEIGHT, WIDTH) * silu_slope(summed)
            if layer_index >= half_depth:
                skip_grads[LAYERS - 1 - layer_index] = lax.optimization_barrier(pre_grad.astype(jnp.bfloat16))
            carried = lax.optimization_barrier((upstream + pre_grad).astype(jnp.bfloat16))
    return jnp.stack(weight_grads)
```

```python
import jax
import jax.numpy as jnp
from jax import lax
from jax.experimental import pallas as pl
from jax.experimental.pallas import tpu as pltpu
from jax.sharding import Mesh, PartitionSpec as P

F32 = jnp.float32
BF16 = jnp.bfloat16
LAYERS = 8
CELLS = 128
TAPS = [(df, dh, dw) for df in (-1, 0, 1) for dh in (-1, 0, 1) for dw in (-1, 0, 1)]
PLACE = [2 * l if l < 4 else 15 - 2 * l for l in range(LAYERS)]


def shifted(source, move):
    df, dh, dw = move
    if move == (0, 0, 0):
        return source
    lane = lax.broadcasted_iota(jnp.int32, (1, CELLS), 1)
    f, h, w = lane // 32 + df, (lane // 8) % 4 + dh, lane % 8 + dw
    inside = (f >= 0) & (f < 4) & (h >= 0) & (h < 4) & (w >= 0) & (w < 8)
    turned = pltpu.roll(source, (-(32 * df + 8 * dh + dw)) % CELLS, 1)
    return jnp.where(inside, turned, 0.0)


def forward_kernel(x_ref, skip_ref, w_ref, act_ref, out_ref):
    summed = x_ref[...].astype(F32) + skip_ref[...].astype(F32)
    act = (summed * jax.nn.sigmoid(summed)).astype(BF16)
    act_ref[...] = act
    act = act.astype(F32)
    total = None
    for first in range(0, 27, 3):
        stacked = jnp.concatenate(
            [shifted(act, TAPS[k]).astype(BF16) for k in range(first, first + 3)], axis=0
        )
        matrix = jnp.concatenate(
            [w_ref[:, k].reshape(512, 256) for k in range(first, first + 3)], axis=1
        )
        part = lax.dot_general(
            matrix, stacked, (((1,), (0,)), ((), ())), preferred_element_type=F32
        )
        total = part if total is None else total + part
    out_ref[...] = total


def backward_kernel(g_ref, up_ref, x_ref, skip_ref, w_ref, sent_ref, pre_ref, pad_ref):
    grads = g_ref[...].astype(F32).T
    column = lax.broadcasted_iota(jnp.int32, (CELLS, 1), 0) % 8
    pad_ref[...] = jnp.zeros(pad_ref.shape, F32)
    for slot, move in enumerate((1, 0, -1)):
        turned = grads
        if move:
            turned = pltpu.roll(grads, (-move) % CELLS, 0)
            turned = jnp.where((column + move >= 0) & (column + move < 8), turned, 0.0)
        pad_ref[slot, 1:5, 1:5] = turned.reshape(4, 4, 8, 512)
    total = None
    for k, (df, dh, dw) in enumerate(TAPS):
        window = pad_ref[dw + 1, 1 - df : 5 - df, 1 - dh : 5 - dh]
        part = lax.dot_general(
            window.reshape(CELLS, 512).astype(BF16),
            w_ref[:, k].reshape(512, 256),
            (((1,), (0,)), ((), ())),
            preferred_element_type=F32,
        )
        total = part if total is None else total + part
    summed = x_ref[...].astype(F32) + skip_ref[...].astype(F32)
    sig = jax.nn.sigmoid(summed)
    pre = total.T * (sig * (1.0 + summed * (1.0 - sig)))
    pre_ref[...] = pre.astype(BF16)
    sent_ref[...] = (up_ref[...] + pre).astype(BF16)


def weight_grad_kernel(g_ref, a_ref, out_ref):
    total = None
    for v in range(0, 32, 2):
        rows = []
        for u in (v, v + 1):
            grads = g_ref[u].astype(F32)
            rows.append(
                jnp.concatenate(
                    [shifted(grads, tuple(-m for m in move)).astype(BF16) for move in TAPS], axis=0
                )
            )
        left = jnp.concatenate(rows, axis=1)
        right = jnp.concatenate([a_ref[v], a_ref[v + 1]], axis=1)
        part = lax.dot_general(
            left, right, (((1,), (1,)), ((), ())), preferred_element_type=F32
        )
        total = part if total is None else total + part
    out_ref[...] = total.astype(BF16)


def own_half(array, core):
    half = array.shape[0] // 2
    return lax.dynamic_slice_in_dim(array, core * half, half, axis=0)


def volume_half(pair, core, x, mirrored):
    picked = [jnp.where(x % 2 == 0, pair[0], pair[1]), jnp.where(x % 2 == 0, pair[1], pair[0])]
    got = []
    for turn in range(2):
        route = []
        for z in range(8):
            for c in range(2):
                for at in range(4):
                    source = (z * 2 + c) * 4 + at
                    micro = at % 2 if turn == 0 else 1 - at % 2
                    target_z = 7 - z if mirrored else z
                    route.append((source, (target_z * 2 + at // 2) * 4 + 2 * micro + c))
        got.append(lax.ppermute(picked[turn], ("zl", "core", "x"), route))
    low = x // 2 == 0
    return jnp.concatenate(
        [jnp.where(low, got[0], got[1]), jnp.where(low, got[1], got[0])], axis=0
    )


def other_partial(partial, core):
    both = lax.all_gather(partial.astype(BF16), "core", axis=0, tiled=False)
    return own_half(jnp.where(core == 0, both[1], both[0]), core)


def on_device(clips, weights, cotangents):
    y, zh, core, x = (lax.axis_index(a) for a in ("y", "zh", "core", "x"))
    layer = jnp.where(zh == 0, y, 7 - y)
    section = ("y", "zh")

    own = lax.all_to_all(
        weights[0].transpose(1, 0, 2).reshape(27, 8, 2, 256), "core", split_axis=2, concat_axis=1
    ).reshape(27, 16, 256)
    own = lax.ppermute(own, section, [(l, PLACE[l]) for l in range(LAYERS)])
    kernel = lax.all_gather(own, "zl", axis=0, tiled=False)
    kernel = lax.all_gather(kernel, "x", axis=0, tiled=False).reshape(32, 27, 16, 256)

    x_hold = volume_half(clips, core, x, False)
    carried = volume_half(cotangents, core, x, True)

    tile = jax.ShapeDtypeStruct((256, CELLS), BF16)
    forward = pl.pallas_call(
        forward_kernel,
        out_shape=(tile, jax.ShapeDtypeStruct((512, CELLS), F32)),
        name="conv_forward",
    )
    backward = pl.pallas_call(
        backward_kernel,
        out_shape=(tile, tile),
        scratch_shapes=(pltpu.VMEM((3, 6, 6, 8, 512), F32),),
        name="conv_backward",
    )
    across = [(z, 15 - z) for z in range(8)]

    skip = jnp.zeros((256, CELLS), BF16)
    for l in range(LAYERS):
        act, partial = forward(x_hold, skip, kernel)
        if l == LAYERS - 1:
            break
        update = own_half(partial, core) + other_partial(partial, core).astype(F32)
        out = (x_hold.astype(F32) + update).astype(BF16)
        if l == 3:
            skip = lax.ppermute(out, ("zh", "zl"), across)
            x_hold = jnp.where(layer == 4, skip, x_hold)
        else:
            got = lax.ppermute(out, section, [(PLACE[l], PLACE[l + 1])])
            x_hold = jnp.where(layer == l + 1, got, x_hold)

    acts = lax.all_gather(act, "zl", axis=0, tiled=False)
    acts = lax.all_gather(acts, "x", axis=0, tiled=False).reshape(32, 256, CELLS)

    back = [(b, a) for a, b in across]
    upstream = carried.astype(F32)
    for l in reversed(range(LAYERS)):
        low = upstream.astype(BF16)
        grads = lax.all_gather(low, "core", axis=0, tiled=True)
        if l == 0:
            break
        sent, pre = backward(grads, upstream, x_hold, skip, kernel)
        if l == 4:
            both = lax.ppermute(jnp.stack([sent, pre]), ("zh", "zl"), back)
            gskip = both[1].astype(F32)
            upstream = jnp.where(layer < 4, gskip, upstream)
            upstream = jnp.where(layer == 3, both[0].astype(F32) + gskip, upstream)
        else:
            got = lax.ppermute(sent, section, [(PLACE[l], PLACE[l - 1])]).astype(F32)
            if l < 4:
                got = got + gskip
            upstream = jnp.where(layer == l - 1, got, upstream)

    rows = grads.reshape(4, 8, 16, CELLS)
    rows = lax.all_to_all(rows, "x", split_axis=0, concat_axis=0)
    rows = lax.all_to_all(rows, "zl", split_axis=1, concat_axis=1).reshape(32, 16, CELLS)
    total = pl.pallas_call(
        weight_grad_kernel,
        out_shape=jax.ShapeDtypeStruct((432, 256), BF16),
        name="weight_grad",
    )(rows, acts)
    total = lax.all_to_all(
        total.reshape(27, 2, 8, 256), "core", split_axis=1, concat_axis=1
    )
    total = lax.ppermute(total, section, [(PLACE[l], l) for l in range(LAYERS)])
    return total.transpose(2, 0, 1, 3).reshape(1, 8, 27, 512).astype(F32)


def solution(mesh):
    fine = Mesh(mesh.devices.reshape(4, 2, 8, 2, 4), ("y", "zh", "zl", "core", "x"))
    placed = (
        P(None, "x", ("zl", "core")),
        P(("y", "zh"), ("x", "zl", "core"), None, None),
        P(None, "x", ("zl", "core")),
    )
    return jax.shard_map(
        on_device,
        mesh=fine,
        in_specs=placed,
        out_specs=P(("y", "zh"), ("x", "zl", "core"), None, None),
        check_vma=False,
    )
```

```python
import jax
import jax.numpy as jnp
from jax import lax
from jax.experimental import pallas as pl
from jax.experimental.pallas import tpu as pltpu
from jax.sharding import Mesh, PartitionSpec as P

F32 = jnp.float32
BF16 = jnp.bfloat16
LAYERS = 8
CELLS = 128
TAPS = [(df, dh, dw) for df in (-1, 0, 1) for dh in (-1, 0, 1) for dw in (-1, 0, 1)]
PLACE = [2 * l if l < 4 else 15 - 2 * l for l in range(LAYERS)]


def shifted(source, move):
    df, dh, dw = move
    if move == (0, 0, 0):
        return source
    lane = lax.broadcasted_iota(jnp.int32, (1, CELLS), 1)
    f, h, w = lane // 32 + df, (lane // 8) % 4 + dh, lane % 8 + dw
    inside = (f >= 0) & (f < 4) & (h >= 0) & (h < 4) & (w >= 0) & (w < 8)
    turned = pltpu.roll(source, (-(32 * df + 8 * dh + dw)) % CELLS, 1)
    return jnp.where(inside, turned, 0.0)


def conv(matrix_of, stacks):
    total = None
    for j, stacked in enumerate(stacks):
        part = lax.dot_general(
            matrix_of(3 * j), stacked, (((1,), (0,)), ((), ())), preferred_element_type=F32
        )
        total = part if total is None else total + part
    return total


def forward_kernel(core_ref, x_ref, skip_ref, w_ref, act_ref, own_ref, other_ref):
    core = core_ref[0]
    summed = x_ref[...].astype(F32) + skip_ref[...].astype(F32)
    act = (summed * jax.nn.sigmoid(summed)).astype(BF16)
    act_ref[...] = act
    act = act.astype(F32)
    stacks = [
        jnp.concatenate(
            [shifted(act, TAPS[k]).astype(BF16) for k in range(first, first + 3)], axis=0
        )
        for first in range(0, 27, 3)
    ]

    def rows(half):
        def matrix_of(first):
            return jnp.concatenate(
                [
                    w_ref[pl.ds(half * 16, 16), k].reshape(256, 256)
                    for k in range(first, first + 3)
                ],
                axis=1,
            )

        return conv(matrix_of, stacks)

    other_ref[...] = rows(1 - core).astype(BF16)
    own_ref[...] = rows(core)


def backward_kernel(g_ref, up_ref, gskip_ref, x_ref, skip_ref, w_ref, sent_ref, pre_ref, pad_ref):
    grads = g_ref[...].astype(F32).T
    column = lax.broadcasted_iota(jnp.int32, (CELLS, 1), 0) % 8
    pad_ref[...] = jnp.zeros(pad_ref.shape, F32)
    for slot, move in enumerate((1, 0, -1)):
        turned = grads
        if move:
            turned = pltpu.roll(grads, (-move) % CELLS, 0)
            turned = jnp.where((column + move >= 0) & (column + move < 8), turned, 0.0)
        pad_ref[slot, 1:5, 1:5] = turned.reshape(4, 4, 8, 512)
    total = None
    for k, (df, dh, dw) in enumerate(TAPS):
        window = pad_ref[dw + 1, 1 - df : 5 - df, 1 - dh : 5 - dh]
        part = lax.dot_general(
            window.reshape(CELLS, 512).astype(BF16),
            w_ref[:, k].reshape(512, 256),
            (((1,), (0,)), ((), ())),
            preferred_element_type=F32,
        )
        total = part if total is None else total + part
    summed = x_ref[...].astype(F32) + skip_ref[...].astype(F32)
    sig = jax.nn.sigmoid(summed)
    pre = total.T * (sig * (1.0 + summed * (1.0 - sig)))
    pre_ref[...] = pre.astype(BF16)
    upstream = up_ref[...].astype(F32) + gskip_ref[...].astype(F32)
    sent_ref[...] = (upstream + pre).astype(BF16)


def weight_grad_kernel(x_ref, g_ref, a_ref, out_ref):
    x = x_ref[0]
    total = None
    for z in range(8):
        for pair in range(2):
            left, right = [], []
            for column in (2 * pair, 2 * pair + 1):
                grads = g_ref[column * 8 + z].astype(F32)
                left.append(
                    jnp.concatenate(
                        [shifted(grads, tuple(-m for m in move)).astype(BF16) for move in TAPS],
                        axis=0,
                    )
                )
                right.append(a_ref[z, (x - column + 4) % 4])
            part = lax.dot_general(
                jnp.concatenate(left, axis=1),
                jnp.concatenate(right, axis=1),
                (((1,), (1,)), ((), ())),
                preferred_element_type=F32,
            )
            total = part if total is None else total + part
    out_ref[...] = total.astype(BF16)


def own_half(array, core):
    half = array.shape[0] // 2
    return lax.dynamic_slice_in_dim(array, core * half, half, axis=0)


def volume_half(pair, core, x, mirrored):
    picked = [jnp.where(x % 2 == 0, pair[0], pair[1]), jnp.where(x % 2 == 0, pair[1], pair[0])]
    got = []
    for turn in range(2):
        route = []
        for z in range(8):
            for c in range(2):
                for at in range(4):
                    source = (z * 2 + c) * 4 + at
                    micro = at % 2 if turn == 0 else 1 - at % 2
                    target_z = 7 - z if mirrored else z
                    route.append((source, (target_z * 2 + at // 2) * 4 + 2 * micro + c))
        got.append(lax.ppermute(picked[turn], ("zl", "core", "x"), route))
    low = x // 2 == 0
    return jnp.concatenate(
        [jnp.where(low, got[0], got[1]), jnp.where(low, got[1], got[0])], axis=0
    )


def near(*arrays):
    return [pltpu.with_memory_space_constraint(array, pltpu.VMEM) for array in arrays]


def on_device(clips, weights, cotangents):
    y, zh, core, x = (lax.axis_index(a) for a in ("y", "zh", "core", "x"))
    layer = jnp.where(zh == 0, y, 7 - y)
    section = ("y", "zh")

    own = lax.all_to_all(
        weights[0].transpose(1, 0, 2).reshape(27, 8, 2, 256), "core", split_axis=2, concat_axis=1
    ).reshape(27, 16, 256)
    own = lax.ppermute(own, section, [(l, PLACE[l]) for l in range(LAYERS)])
    kernel = lax.all_gather(own, "zl", axis=0, tiled=False)
    kernel = lax.all_gather(kernel, "x", axis=0, tiled=False).reshape(32, 27, 16, 256)

    x_hold = volume_half(clips, core, x, False)
    carried = volume_half(cotangents, core, x, True)

    kernel = near(kernel)[0]
    tile = pltpu.VMEM((256, CELLS), BF16)
    limits = pltpu.CompilerParams(vmem_limit_bytes=20 * 1024 * 1024)
    everywhere = pl.BlockSpec(memory_space=pltpu.VMEM)
    scalar = pl.BlockSpec(memory_space=pltpu.SMEM)
    forward = pl.pallas_call(
        forward_kernel,
        in_specs=[scalar] + [everywhere] * 3,
        out_shape=(tile, pltpu.VMEM((256, CELLS), F32), tile),
        compiler_params=limits,
        name="conv_forward",
    )
    backward = pl.pallas_call(
        backward_kernel,
        out_shape=(tile, tile),
        scratch_shapes=(pltpu.VMEM((3, 6, 6, 8, 512), F32),),
        compiler_params=limits,
        name="conv_backward",
    )
    core_at = core.astype(jnp.int32).reshape(1)
    across = [(z, 15 - z) for z in range(8)]

    skip = jnp.zeros((256, CELLS), BF16)
    for l in range(LAYERS):
        act, mine, other = forward(core_at, *near(x_hold, skip, kernel))
        if l == LAYERS - 1:
            break
        both = lax.all_gather(other, "core", axis=0, tiled=False)
        update = mine + jnp.where(core == 0, both[1], both[0]).astype(F32)
        out = (x_hold.astype(F32) + update).astype(BF16)
        if l == 3:
            skip = lax.ppermute(out, ("zh", "zl"), across)
            x_hold = jnp.where(layer == 4, skip, x_hold)
        else:
            got = lax.ppermute(out, section, [(PLACE[l], PLACE[l + 1])])
            x_hold = jnp.where(layer == l + 1, got, x_hold)

    acts = jnp.stack(
        [act] + [lax.ppermute(act, "x", [(i, (i + turn) % 4) for i in range(4)]) for turn in (1, 2, 3)]
    )
    acts = lax.all_gather(acts, "zl", axis=0, tiled=False)

    back = [(b, a) for a, b in across]
    gskip = jnp.zeros((256, CELLS), BF16)
    for l in reversed(range(LAYERS)):
        low = (carried.astype(F32) + gskip.astype(F32)).astype(BF16)
        grads = lax.all_gather(low, "core", axis=0, tiled=True)
        if l == 0:
            break
        sent, pre = backward(*near(grads, carried, gskip, x_hold, skip, kernel))
        if l == 4:
            whole = (sent.astype(F32) + pre.astype(F32)).astype(BF16)
            got = lax.ppermute(jnp.where(layer == 4, whole, pre), ("zh", "zl"), back)
            carried = jnp.where(layer == 3, got, carried)
            gskip = jnp.where(layer < 3, got, gskip)
        else:
            got = lax.ppermute(sent, section, [(PLACE[l], PLACE[l - 1])])
            carried = jnp.where(layer == l - 1, got, carried)

    rows = grads.reshape(4, 8, 16, CELLS)
    rows = lax.all_to_all(rows, "x", split_axis=0, concat_axis=0)
    rows = lax.all_to_all(rows, "zl", split_axis=1, concat_axis=1).reshape(32, 16, CELLS)
    total = pl.pallas_call(
        weight_grad_kernel,
        in_specs=[scalar] + [everywhere] * 2,
        out_shape=pltpu.VMEM((432, 256), BF16),
        compiler_params=limits,
        name="weight_grad",
    )(x.astype(jnp.int32).reshape(1), rows, acts)
    total = lax.all_to_all(
        total.reshape(27, 2, 8, 256), "core", split_axis=1, concat_axis=1
    )
    total = lax.ppermute(total, section, [(PLACE[l], l) for l in range(LAYERS)])
    return total.transpose(2, 0, 1, 3).reshape(1, 8, 27, 512).astype(F32)


def solution(mesh):
    fine = Mesh(mesh.devices.reshape(4, 2, 8, 2, 4), ("y", "zh", "zl", "core", "x"))
    placed = (
        P(None, "x", ("zl", "core")),
        P(("y", "zh"), ("x", "zl", "core"), None, None),
        P(None, "x", ("zl", "core")),
    )
    return jax.shard_map(
        on_device,
        mesh=fine,
        in_specs=placed,
        out_specs=P(("y", "zh"), ("x", "zl", "core"), None, None),
        check_vma=False,
    )
```

```python
import jax
import jax.numpy as jnp
from jax import lax
from jax.experimental import pallas as pl
from jax.experimental.pallas import tpu as pltpu
from jax.sharding import Mesh, PartitionSpec as P

F32 = jnp.float32
BF16 = jnp.bfloat16
LAYERS = 8
CELLS = 128
TAPS = [(df, dh, dw) for df in (-1, 0, 1) for dh in (-1, 0, 1) for dw in (-1, 0, 1)]
PLACE = [2 * l if l < 4 else 15 - 2 * l for l in range(LAYERS)]


def shifted(source, move):
    df, dh, dw = move
    if move == (0, 0, 0):
        return source
    lane = lax.broadcasted_iota(jnp.int32, (1, CELLS), 1)
    f, h, w = lane // 32 + df, (lane // 8) % 4 + dh, lane % 8 + dw
    inside = (f >= 0) & (f < 4) & (h >= 0) & (h < 4) & (w >= 0) & (w < 8)
    turned = pltpu.roll(source, (-(32 * df + 8 * dh + dw)) % CELLS, 1)
    return jnp.where(inside, turned, 0.0)


def conv(matrix_of, stacks):
    total = None
    for j, stacked in enumerate(stacks):
        part = lax.dot_general(
            matrix_of(3 * j), stacked, (((1,), (0,)), ((), ())), preferred_element_type=F32
        )
        total = part if total is None else total + part
    return total


def forward_kernel(core_ref, x_ref, skip_ref, w_ref, act_ref, own_ref, other_ref):
    core = core_ref[0]
    summed = x_ref[...].astype(F32) + skip_ref[...].astype(F32)
    act = (summed * jax.nn.sigmoid(summed)).astype(BF16)
    act_ref[...] = act
    act = act.astype(F32)
    stacks = [
        jnp.concatenate(
            [shifted(act, TAPS[k]).astype(BF16) for k in range(first, first + 3)], axis=0
        )
        for first in range(0, 27, 3)
    ]

    def rows(half):
        def matrix_of(first):
            return jnp.concatenate(
                [
                    w_ref[pl.ds(half * 16, 16), k].reshape(256, 256)
                    for k in range(first, first + 3)
                ],
                axis=1,
            )

        return conv(matrix_of, stacks)

    other_ref[...] = rows(1 - core).astype(BF16)
    own_ref[...] = rows(core)


def backward_kernel(g_ref, up_ref, gskip_ref, x_ref, skip_ref, w_ref, sent_ref, pre_ref, pad_ref):
    grads = g_ref[...].astype(F32).T
    column = lax.broadcasted_iota(jnp.int32, (CELLS, 1), 0) % 8
    pad_ref[...] = jnp.zeros(pad_ref.shape, F32)
    for slot, move in enumerate((1, 0, -1)):
        turned = grads
        if move:
            turned = pltpu.roll(grads, (-move) % CELLS, 0)
            turned = jnp.where((column + move >= 0) & (column + move < 8), turned, 0.0)
        pad_ref[slot, 1:5, 1:5] = turned.reshape(4, 4, 8, 512)
    total = None
    for k, (df, dh, dw) in enumerate(TAPS):
        window = pad_ref[dw + 1, 1 - df : 5 - df, 1 - dh : 5 - dh]
        part = lax.dot_general(
            window.reshape(CELLS, 512).astype(BF16),
            w_ref[:, k].reshape(512, 256),
            (((1,), (0,)), ((), ())),
            preferred_element_type=F32,
        )
        total = part if total is None else total + part
    summed = x_ref[...].astype(F32) + skip_ref[...].astype(F32)
    sig = jax.nn.sigmoid(summed)
    pre = total.T * (sig * (1.0 + summed * (1.0 - sig)))
    pre_ref[...] = pre.astype(BF16)
    upstream = up_ref[...].astype(F32) + gskip_ref[...].astype(F32)
    sent_ref[...] = (upstream + pre).astype(BF16)


DOUBLING = [0, 4, 2, 6, 1, 5, 3, 7]
CHUNKS = 3


def weight_grad_kernel(z_ref, g_ref, a_ref, out_ref):
    z = z_ref[0]
    total = None
    for column in range(4):
        for q in range(0, 8, 2):
            left, right = [], []
            for place in (q, q + 1):
                grads = g_ref[column * 8 + (z ^ DOUBLING[place])].astype(F32)
                left.append(
                    jnp.concatenate(
                        [shifted(grads, tuple(-m for m in move)).astype(BF16) for move in TAPS],
                        axis=0,
                    )
                )
                right.append(a_ref[column, place])
            part = lax.dot_general(
                jnp.concatenate(left, axis=1),
                jnp.concatenate(right, axis=1),
                (((1,), (1,)), ((), ())),
                preferred_element_type=F32,
            )
            total = part if total is None else total + part
    out_ref[...] = total.astype(BF16)


def place_kernel(at_ref, *refs):
    pieces, out_ref, sems = refs[:-2], refs[-2], refs[-1]
    x, z, flip = at_ref[0], at_ref[1], at_ref[2]
    copies = []
    for chunk in range(CHUNKS):
        own, before, after, far_low, far_high = pieces[5 * chunk : 5 * chunk + 5]
        taps = pl.ds(chunk * 27 // CHUNKS, 27 // CHUNKS)
        for q in range(8):
            block = z ^ DOUBLING[q] ^ flip
            far = far_low.at[q] if q < 4 else far_high.at[q - 4]
            for turn, source in enumerate((own.at[q], after.at[q], far, before.at[q])):
                target = ((x + turn) % 4) * 8 + block
                copies.append(
                    pltpu.make_async_copy(source, out_ref.at[target, taps], sems.at[len(copies)])
                )
    for copy in copies:
        copy.start()
    for copy in copies:
        copy.wait()


def volume_half(pair, core, x, mirrored):
    picked = [jnp.where(x % 2 == 0, pair[0], pair[1]), jnp.where(x % 2 == 0, pair[1], pair[0])]
    got = []
    for turn in range(2):
        route = []
        for z in range(8):
            for c in range(2):
                for at in range(4):
                    source = (z * 2 + c) * 4 + at
                    micro = at % 2 if turn == 0 else 1 - at % 2
                    target_z = 7 - z if mirrored else z
                    route.append((source, (target_z * 2 + at // 2) * 4 + 2 * micro + c))
        got.append(lax.ppermute(picked[turn], ("zl", "core", "x"), route))
    low = x // 2 == 0
    return jnp.concatenate(
        [jnp.where(low, got[0], got[1]), jnp.where(low, got[1], got[0])], axis=0
    )


def near(*arrays):
    return [pltpu.with_memory_space_constraint(array, pltpu.VMEM) for array in arrays]


def on_device(clips, weights, cotangents):
    y, zh, z, core, x = (lax.axis_index(a) for a in ("y", "zh", "zl", "core", "x"))
    layer = jnp.where(zh == 0, y, 7 - y)
    flip = jnp.where((layer == 1) | (layer == 3) | (layer == 4) | (layer == 6), 7, 0)
    section = ("y", "zh")
    homes = []
    for l in range(LAYERS):
        for at in range(8):
            to = 7 - at if l in (1, 3, 4, 6) else at
            homes.append((l * 8 + at, PLACE[l] * 8 + to))

    own = lax.all_to_all(
        weights[0].transpose(1, 0, 2).reshape(27, 8, 2, 256), "core", split_axis=2, concat_axis=1
    ).reshape(27, 16, 256)
    own = lax.ppermute(own, ("y", "zh", "zl"), homes)
    x_hold = volume_half(clips, core, x, False)
    carried = volume_half(cotangents, core, x, True)

    def swap(array, bit):
        return lax.ppermute(array, "zl", [(i, i ^ bit) for i in range(8)])

    up = [(i, (i + 1) % 4) for i in range(4)]
    down = [(b, a) for a, b in up]
    pieces = []
    step = 27 // CHUNKS
    for chunk in range(CHUNKS):
        part = own[None, chunk * step : chunk * step + step]
        for bit in (4, 2, 1):
            part = jnp.concatenate([part, swap(part, bit)], axis=0)
        before = lax.ppermute(part, "x", up)
        after = lax.ppermute(part, "x", down)
        far_low = lax.ppermute(before[:4], "x", up)
        far_high = lax.ppermute(after[4:], "x", down)
        pieces += [part, before, after, far_low, far_high]
    everywhere = pl.BlockSpec(memory_space=pltpu.VMEM)
    scalar = pl.BlockSpec(memory_space=pltpu.SMEM)
    limits = pltpu.CompilerParams(vmem_limit_bytes=20 * 1024 * 1024)
    kernel = pl.pallas_call(
        place_kernel,
        in_specs=[scalar] + [pl.BlockSpec(memory_space=pl.ANY)] * len(pieces),
        out_shape=pltpu.VMEM((32, 27, 16, 256), BF16),
        scratch_shapes=(pltpu.SemaphoreType.DMA((32 * CHUNKS,)),),
        compiler_params=limits,
        name="place_kernels",
    )(jnp.stack([x, z, flip]).astype(jnp.int32), *pieces)
    kernel, x_hold, carried = lax.optimization_barrier((kernel, x_hold, carried))

    tile = pltpu.VMEM((256, CELLS), BF16)
    forward = pl.pallas_call(
        forward_kernel,
        in_specs=[scalar] + [everywhere] * 3,
        out_shape=(tile, pltpu.VMEM((256, CELLS), F32), tile),
        compiler_params=limits,
        name="conv_forward",
    )
    backward = pl.pallas_call(
        backward_kernel,
        out_shape=(tile, tile),
        scratch_shapes=(pltpu.VMEM((3, 6, 6, 8, 512), F32),),
        compiler_params=limits,
        name="conv_backward",
    )
    core_at = core.astype(jnp.int32).reshape(1)
    across = [(z, 15 - z) for z in range(8)]

    skip = jnp.zeros((256, CELLS), BF16)
    for l in range(LAYERS):
        act, mine, other = forward(core_at, *near(x_hold, skip, kernel))
        if l == LAYERS - 1:
            break
        both = lax.all_gather(other, "core", axis=0, tiled=False)
        update = mine + jnp.where(core == 0, both[1], both[0]).astype(F32)
        out = (x_hold.astype(F32) + update).astype(BF16)
        if l == 3:
            skip = lax.ppermute(out, ("zh", "zl"), across)
            x_hold = jnp.where(layer == 4, skip, x_hold)
        else:
            got = lax.ppermute(out, section, [(PLACE[l], PLACE[l + 1])])
            x_hold = jnp.where(layer == l + 1, got, x_hold)

    acts = act[None]
    back = [(b, a) for a, b in across]
    gskip = jnp.zeros((256, CELLS), BF16)
    for l in reversed(range(LAYERS)):
        low = (carried.astype(F32) + gskip.astype(F32)).astype(BF16)
        grads = lax.all_gather(low, "core", axis=0, tiled=True)
        if l == 0:
            break
        sent, pre = backward(*near(grads, carried, gskip, x_hold, skip, kernel))
        if l > 4:
            acts, sent = lax.optimization_barrier((acts, sent))
            acts = jnp.concatenate([acts, swap(acts, 1 << (l - 5))], axis=0)
        if l == 4:
            acts, pre = lax.optimization_barrier((acts, pre))
            acts = lax.all_gather(acts, "x", axis=0, tiled=False)
            whole = (sent.astype(F32) + pre.astype(F32)).astype(BF16)
            got = lax.ppermute(jnp.where(layer == 4, whole, pre), ("zh", "zl"), back)
            carried = jnp.where(layer == 3, got, carried)
            gskip = jnp.where(layer < 3, got, gskip)
        else:
            got = lax.ppermute(sent, section, [(PLACE[l], PLACE[l - 1])])
            carried = jnp.where(layer == l - 1, got, carried)

    rows = grads.reshape(4, 8, 16, CELLS)
    rows = jnp.where(flip == 0, rows, rows[:, ::-1])
    rows = lax.all_to_all(rows, "x", split_axis=0, concat_axis=0)
    rows = lax.all_to_all(rows, "zl", split_axis=1, concat_axis=1).reshape(32, 16, CELLS)
    total = pl.pallas_call(
        weight_grad_kernel,
        in_specs=[scalar] + [everywhere] * 2,
        out_shape=pltpu.VMEM((432, 256), BF16),
        compiler_params=limits,
        name="weight_grad",
    )(z.astype(jnp.int32).reshape(1), rows, acts)
    total = lax.all_to_all(
        total.reshape(27, 2, 8, 256), "core", split_axis=1, concat_axis=1
    )
    total = lax.ppermute(total, ("y", "zh", "zl"), [(b, a) for a, b in homes])
    return total.transpose(2, 0, 1, 3).reshape(1, 8, 27, 512).astype(F32)


def solution(mesh):
    fine = Mesh(mesh.devices.reshape(4, 2, 8, 2, 4), ("y", "zh", "zl", "core", "x"))
    placed = (
        P(None, "x", ("zl", "core")),
        P(("y", "zh"), ("x", "zl", "core"), None, None),
        P(None, "x", ("zl", "core")),
    )
    return jax.shard_map(
        on_device,
        mesh=fine,
        in_specs=placed,
        out_specs=P(("y", "zh"), ("x", "zl", "core"), None, None),
        check_vma=False,
    )
```

```python
import jax
import jax.numpy as jnp
from jax import lax
from jax.experimental import pallas as pl
from jax.experimental.pallas import tpu as pltpu
from jax.sharding import Mesh, PartitionSpec as P

F32 = jnp.float32
BF16 = jnp.bfloat16
LAYERS = 8
CELLS = 128
TAPS = [(df, dh, dw) for df in (-1, 0, 1) for dh in (-1, 0, 1) for dw in (-1, 0, 1)]
PLACE = [2 * l if l < 4 else 15 - 2 * l for l in range(LAYERS)]


def shifted(source, move):
    df, dh, dw = move
    if move == (0, 0, 0):
        return source
    lane = lax.broadcasted_iota(jnp.int32, (1, CELLS), 1)
    f, h, w = lane // 32 + df, (lane // 8) % 4 + dh, lane % 8 + dw
    inside = (f >= 0) & (f < 4) & (h >= 0) & (h < 4) & (w >= 0) & (w < 8)
    turned = pltpu.roll(source, (-(32 * df + 8 * dh + dw)) % CELLS, 1)
    return jnp.where(inside, turned, 0.0)


DOUBLING = [0, 4, 2, 6, 1, 5, 3, 7]
CHUNKS = 3
PIECES = 5 * CHUNKS


def arrival_blocks(at_ref):
    x, z, flip = at_ref[1], at_ref[2], at_ref[3]
    return [((x + turn) % 4) * 8 + (z ^ place ^ flip) for turn in range(4) for place in DOUBLING]


def tap_rows(pieces, k):
    own, before, after, far_low, far_high = pieces[5 * (k // 9) : 5 * (k // 9) + 5]
    order = (own, after, far_low, far_high, before)
    return jnp.concatenate([piece[:, k % 9].reshape(-1, 256) for piece in order], axis=0)


def forward_kernel(at_ref, x_ref, skip_ref, *refs):
    pieces, (act_ref, own_ref, other_ref, rows_ref) = refs[:PIECES], refs[PIECES:]
    core = at_ref[0]
    summed = x_ref[...].astype(F32) + skip_ref[...].astype(F32)
    act = (summed * jax.nn.sigmoid(summed)).astype(BF16)
    act_ref[...] = act
    act = act.astype(F32)
    total = None
    for first in range(0, 27, 3):
        taps = range(first, first + 3)
        part = lax.dot_general(
            jnp.concatenate([tap_rows(pieces, k) for k in taps], axis=1),
            jnp.concatenate([shifted(act, TAPS[k]).astype(BF16) for k in taps], axis=0),
            (((1,), (0,)), ((), ())),
            preferred_element_type=F32,
        )
        total = part if total is None else total + part
    for place, block in enumerate(arrival_blocks(at_ref)):
        rows_ref[pl.ds(pl.multiple_of(block * 16, 16), 16)] = total[place * 16 : place * 16 + 16]
    own_ref[...] = rows_ref[pl.ds(pl.multiple_of(core * 256, 256), 256)]
    other_ref[...] = rows_ref[pl.ds(pl.multiple_of((1 - core) * 256, 256), 256)].astype(BF16)


def backward_kernel(at_ref, g_ref, up_ref, gskip_ref, x_ref, skip_ref, *refs):
    pieces, (sent_ref, pre_ref, pad_ref) = refs[:PIECES], refs[PIECES:]
    grads = jnp.concatenate(
        [g_ref[pl.ds(pl.multiple_of(b * 16, 16), 16)] for b in arrival_blocks(at_ref)], axis=0
    )
    grads = grads.astype(F32).T
    column = lax.broadcasted_iota(jnp.int32, (CELLS, 1), 0) % 8
    pad_ref[...] = jnp.zeros(pad_ref.shape, F32)
    for slot, move in enumerate((1, 0, -1)):
        turned = grads
        if move:
            turned = pltpu.roll(grads, (-move) % CELLS, 0)
            turned = jnp.where((column + move >= 0) & (column + move < 8), turned, 0.0)
        pad_ref[slot, 1:5, 1:5] = turned.reshape(4, 4, 8, 512)
    total = None
    for k, (df, dh, dw) in enumerate(TAPS):
        window = pad_ref[dw + 1, 1 - df : 5 - df, 1 - dh : 5 - dh]
        part = lax.dot_general(
            window.reshape(CELLS, 512).astype(BF16),
            tap_rows(pieces, k),
            (((1,), (0,)), ((), ())),
            preferred_element_type=F32,
        )
        total = part if total is None else total + part
    summed = x_ref[...].astype(F32) + skip_ref[...].astype(F32)
    sig = jax.nn.sigmoid(summed)
    pre = total.T * (sig * (1.0 + summed * (1.0 - sig)))
    pre_ref[...] = pre.astype(BF16)
    upstream = up_ref[...].astype(F32) + gskip_ref[...].astype(F32)
    sent_ref[...] = (upstream + pre).astype(BF16)


def weight_grad_kernel(at_ref, g_ref, a_ref, out_ref):
    z = at_ref[2]
    total = None
    for column in range(4):
        for q in range(0, 8, 2):
            left, right = [], []
            for place in (q, q + 1):
                grads = g_ref[column * 8 + (z ^ DOUBLING[place])].astype(F32)
                left.append(
                    jnp.concatenate(
                        [shifted(grads, tuple(-m for m in move)).astype(BF16) for move in TAPS],
                        axis=0,
                    )
                )
                right.append(a_ref[column, place])
            part = lax.dot_general(
                jnp.concatenate(left, axis=1),
                jnp.concatenate(right, axis=1),
                (((1,), (1,)), ((), ())),
                preferred_element_type=F32,
            )
            total = part if total is None else total + part
    out_ref[...] = total.astype(BF16)


def volume_half(pair, core, x, mirrored):
    picked = [jnp.where(x % 2 == 0, pair[0], pair[1]), jnp.where(x % 2 == 0, pair[1], pair[0])]
    got = []
    for turn in range(2):
        route = []
        for z in range(8):
            for c in range(2):
                for at in range(4):
                    source = (z * 2 + c) * 4 + at
                    micro = at % 2 if turn == 0 else 1 - at % 2
                    target_z = 7 - z if mirrored else z
                    route.append((source, (target_z * 2 + at // 2) * 4 + 2 * micro + c))
        got.append(lax.ppermute(picked[turn], ("zl", "core", "x"), route))
    low = x // 2 == 0
    return jnp.concatenate(
        [jnp.where(low, got[0], got[1]), jnp.where(low, got[1], got[0])], axis=0
    )


def near(*arrays):
    return [pltpu.with_memory_space_constraint(array, pltpu.VMEM) for array in arrays]


def on_device(clips, weights, cotangents):
    y, zh, z, core, x = (lax.axis_index(a) for a in ("y", "zh", "zl", "core", "x"))
    layer = jnp.where(zh == 0, y, 7 - y)
    flip = jnp.where((layer == 1) | (layer == 3) | (layer == 4) | (layer == 6), 7, 0)
    section = ("y", "zh")
    homes = []
    for l in range(LAYERS):
        for at in range(8):
            to = 7 - at if l in (1, 3, 4, 6) else at
            homes.append((l * 8 + at, PLACE[l] * 8 + to))

    own = lax.all_to_all(
        weights[0].transpose(1, 0, 2).reshape(27, 8, 2, 256), "core", split_axis=2, concat_axis=1
    ).reshape(27, 16, 256)
    x_hold = volume_half(clips, core, x, False)
    carried = volume_half(cotangents, core, x, True)
    own, x_hold, carried = lax.optimization_barrier((own, x_hold, carried))

    def swap(array, bit):
        return lax.ppermute(array, "zl", [(i, i ^ bit) for i in range(8)])

    up = [(i, (i + 1) % 4) for i in range(4)]
    down = [(b, a) for a, b in up]
    pieces = []
    step = 27 // CHUNKS
    for chunk in range(CHUNKS):
        part = own[None, chunk * step : chunk * step + step]
        part = lax.ppermute(part, ("y", "zh", "zl"), homes)
        for bit in (4, 2, 1):
            part = jnp.concatenate([part, swap(part, bit)], axis=0)
        before = lax.ppermute(part, "x", up)
        after = lax.ppermute(part, "x", down)
        far_low = lax.ppermute(before[:4], "x", up)
        far_high = lax.ppermute(after[4:], "x", down)
        pieces += [part, before, after, far_low, far_high]
    everywhere = pl.BlockSpec(memory_space=pltpu.VMEM)
    scalar = pl.BlockSpec(memory_space=pltpu.SMEM)
    limits = pltpu.CompilerParams(vmem_limit_bytes=20 * 1024 * 1024)
    at = jnp.stack([core, x, z, flip]).astype(jnp.int32)

    tile = pltpu.VMEM((256, CELLS), BF16)
    forward = pl.pallas_call(
        forward_kernel,
        in_specs=[scalar] + [everywhere] * (2 + PIECES),
        out_shape=(tile, pltpu.VMEM((256, CELLS), F32), tile),
        scratch_shapes=(pltpu.VMEM((512, CELLS), F32),),
        compiler_params=limits,
        name="conv_forward",
    )
    backward = pl.pallas_call(
        backward_kernel,
        in_specs=[scalar] + [everywhere] * (5 + PIECES),
        out_shape=(tile, tile),
        scratch_shapes=(pltpu.VMEM((3, 6, 6, 8, 512), F32),),
        compiler_params=limits,
        name="conv_backward",
    )
    across = [(i, 15 - i) for i in range(8)]

    skip = jnp.zeros((256, CELLS), BF16)
    for l in range(LAYERS):
        act, mine, other = forward(at, *near(x_hold, skip, *pieces))
        if l == LAYERS - 1:
            break
        both = lax.all_gather(other, "core", axis=0, tiled=False)
        update = mine + jnp.where(core == 0, both[1], both[0]).astype(F32)
        out = (x_hold.astype(F32) + update).astype(BF16)
        if l == 3:
            skip = lax.ppermute(out, ("zh", "zl"), across)
            x_hold = jnp.where(layer == 4, skip, x_hold)
        else:
            got = lax.ppermute(out, section, [(PLACE[l], PLACE[l + 1])])
            x_hold = jnp.where(layer == l + 1, got, x_hold)

    acts = act[None]
    back = [(b, a) for a, b in across]
    gskip = jnp.zeros((256, CELLS), BF16)
    for l in reversed(range(LAYERS)):
        low = (carried.astype(F32) + gskip.astype(F32)).astype(BF16)
        grads = lax.all_gather(low, "core", axis=0, tiled=True)
        if l == 0:
            break
        sent, pre = backward(at, *near(grads, carried, gskip, x_hold, skip, *pieces))
        if l > 4:
            acts, sent = lax.optimization_barrier((acts, sent))
            acts = jnp.concatenate([acts, swap(acts, 1 << (l - 5))], axis=0)
        if l == 4:
            acts, pre = lax.optimization_barrier((acts, pre))
            acts = lax.all_gather(acts, "x", axis=0, tiled=False)
            whole = (sent.astype(F32) + pre.astype(F32)).astype(BF16)
            got = lax.ppermute(jnp.where(layer == 4, whole, pre), ("zh", "zl"), back)
            carried = jnp.where(layer == 3, got, carried)
            gskip = jnp.where(layer < 3, got, gskip)
        else:
            got = lax.ppermute(sent, section, [(PLACE[l], PLACE[l - 1])])
            carried = jnp.where(layer == l - 1, got, carried)

    rows = grads.reshape(4, 8, 16, CELLS)
    rows = jnp.where(flip == 0, rows, rows[:, ::-1])
    rows = lax.all_to_all(rows, "x", split_axis=0, concat_axis=0)
    rows = lax.all_to_all(rows, "zl", split_axis=1, concat_axis=1).reshape(32, 16, CELLS)
    total = pl.pallas_call(
        weight_grad_kernel,
        in_specs=[scalar] + [everywhere] * 2,
        out_shape=pltpu.VMEM((432, 256), BF16),
        compiler_params=limits,
        name="weight_grad",
    )(at, rows, acts)
    total = lax.all_to_all(
        total.reshape(27, 2, 8, 256), "core", split_axis=1, concat_axis=1
    )
    total = lax.ppermute(total, ("y", "zh", "zl"), [(b, a) for a, b in homes])
    return total.transpose(2, 0, 1, 3).reshape(1, 8, 27, 512).astype(F32)


def solution(mesh):
    fine = Mesh(mesh.devices.reshape(4, 2, 8, 2, 4), ("y", "zh", "zl", "core", "x"))
    placed = (
        P(None, "x", ("zl", "core")),
        P(("y", "zh"), ("x", "zl", "core"), None, None),
        P(None, "x", ("zl", "core")),
    )
    return jax.shard_map(
        on_device,
        mesh=fine,
        in_specs=placed,
        out_specs=P(("y", "zh"), ("x", "zl", "core"), None, None),
        check_vma=False,
    )
```

```python
import jax
import jax.numpy as jnp
from jax import lax
from jax.experimental import pallas as pl
from jax.experimental.pallas import tpu as pltpu
from jax.sharding import Mesh, PartitionSpec as P

F32 = jnp.float32
BF16 = jnp.bfloat16
LAYERS = 8
CELLS = 128
TAPS = [(df, dh, dw) for df in (-1, 0, 1) for dh in (-1, 0, 1) for dw in (-1, 0, 1)]
PARITY = [0, 1, 1, 0, 0, 1, 1, 0]
PLACE = [l // 2 * 2 + PARITY[l] for l in range(LAYERS)]
EDGES = (0, 15, 27)
CHUNKS = len(EDGES) - 1
OFFSETS = [0, 8, 4, 12, 2, 6, 14, 10]
PLANE = ("zh", "zq", "zp")


def serves_low(y, z):
    return (y + z) % 2 == 0


def block_of(low, z):
    return jnp.where(low, jnp.where(z < 8, z, 15 - z), jnp.where(z >= 8, z - 8, 7 - z))


EXCHANGE = [
    (y * 16 + z, y * 16 + 15 - z)
    for y in range(4)
    for z in range(16)
    if serves_low(y, z) != (z < 8)
]


def shifted(source, move):
    df, dh, dw = move
    if move == (0, 0, 0):
        return source
    lane = lax.broadcasted_iota(jnp.int32, (1, CELLS), 1)
    f, h, w = lane // 32 + df, (lane // 8) % 4 + dh, lane % 8 + dw
    inside = (f >= 0) & (f < 4) & (h >= 0) & (h < 4) & (w >= 0) & (w < 8)
    turned = pltpu.roll(source, (-(32 * df + 8 * dh + dw)) % CELLS, 1)
    return jnp.where(inside, turned, 0.0)


def tap_rows(kernels, k):
    chunk = max(c for c in range(CHUNKS) if EDGES[c] <= k)
    return kernels[chunk][:, k - EDGES[chunk]].reshape(512, 256)


def place_kernel(at_ref, own, before, after, far_low, far_high, out_ref, sems):
    x, z, low = at_ref[1], at_ref[2], at_ref[3]
    copies = []
    for q, offset in enumerate(OFFSETS):
        block = block_of(low == 1, (z + offset) % 16)
        far = far_low.at[q] if q < 4 else far_high.at[q - 4]
        for turn, source in enumerate((own.at[q], after.at[q], far, before.at[q])):
            target = ((x + turn) % 4) * 8 + block
            copies.append(pltpu.make_async_copy(source, out_ref.at[target], sems.at[len(copies)]))
    for copy in copies:
        copy.start()
    for copy in copies:
        copy.wait()


def forward_kernel(at_ref, x_ref, skip_ref, *refs):
    kernels, (act_ref, own_ref, other_ref, rows_ref) = refs[:CHUNKS], refs[CHUNKS:]
    core = at_ref[0]
    summed = x_ref[...].astype(F32) + skip_ref[...].astype(F32)
    act = (summed * jax.nn.sigmoid(summed)).astype(BF16)
    act_ref[...] = act
    act = act.astype(F32)
    total = None
    for first in range(0, 27, 3):
        taps = range(first, first + 3)
        part = lax.dot_general(
            jnp.concatenate([tap_rows(kernels, k) for k in taps], axis=1),
            jnp.concatenate([shifted(act, TAPS[k]).astype(BF16) for k in taps], axis=0),
            (((1,), (0,)), ((), ())),
            preferred_element_type=F32,
        )
        total = part if total is None else total + part
    rows_ref[...] = total
    own_ref[...] = rows_ref[pl.ds(pl.multiple_of(core * 256, 256), 256)]
    other_ref[...] = rows_ref[pl.ds(pl.multiple_of((1 - core) * 256, 256), 256)].astype(BF16)


def backward_kernel(g_ref, up_ref, gskip_ref, x_ref, skip_ref, *refs):
    kernels, (sent_ref, pre_ref, pad_ref) = refs[:CHUNKS], refs[CHUNKS:]
    grads = g_ref[...].astype(F32).T
    column = lax.broadcasted_iota(jnp.int32, (CELLS, 1), 0) % 8
    pad_ref[...] = jnp.zeros(pad_ref.shape, F32)
    for slot, move in enumerate((1, 0, -1)):
        turned = grads
        if move:
            turned = pltpu.roll(grads, (-move) % CELLS, 0)
            turned = jnp.where((column + move >= 0) & (column + move < 8), turned, 0.0)
        pad_ref[slot, 1:5, 1:5] = turned.reshape(4, 4, 8, 512)
    total = None
    for k, (df, dh, dw) in enumerate(TAPS):
        window = pad_ref[dw + 1, 1 - df : 5 - df, 1 - dh : 5 - dh]
        part = lax.dot_general(
            window.reshape(CELLS, 512).astype(BF16),
            tap_rows(kernels, k),
            (((1,), (0,)), ((), ())),
            preferred_element_type=F32,
        )
        total = part if total is None else total + part
    summed = x_ref[...].astype(F32) + skip_ref[...].astype(F32)
    sig = jax.nn.sigmoid(summed)
    pre = total.T * (sig * (1.0 + summed * (1.0 - sig)))
    pre_ref[...] = pre.astype(BF16)
    upstream = up_ref[...].astype(F32) + gskip_ref[...].astype(F32)
    sent_ref[...] = (upstream + pre).astype(BF16)


def weight_grad_kernel(at_ref, g_ref, own, before, after, far_low, far_high, out_ref):
    x, z = at_ref[1], at_ref[2]
    total = None
    for turn, piece in enumerate((own, after, None, before)):
        for q in range(0, 8, 2):
            left, right = [], []
            for place in (q, q + 1):
                row = ((x + turn) % 4) * 8 + ((z + OFFSETS[place]) % 16) // 2
                grads = g_ref[row].astype(F32)
                left.append(
                    jnp.concatenate(
                        [shifted(grads, tuple(-m for m in move)).astype(BF16) for move in TAPS],
                        axis=0,
                    )
                )
                if piece is not None:
                    right.append(piece[place])
                else:
                    right.append(far_low[place] if place < 4 else far_high[place - 4])
            part = lax.dot_general(
                jnp.concatenate(left, axis=1),
                jnp.concatenate(right, axis=1),
                (((1,), (1,)), ((), ())),
                preferred_element_type=F32,
            )
            total = part if total is None else total + part
    out_ref[...] = total.astype(BF16)


def volume_half(pair, x, y):
    picked = [jnp.where(x % 2 == 0, pair[0], pair[1]), jnp.where(x % 2 == 0, pair[1], pair[0])]
    got = []
    for turn in range(2):
        route = []
        for place in range(8):
            source_z = 2 * place if place < 4 else 2 * place + 1
            for c in range(2):
                for at in range(4):
                    source = ((y * 16 + source_z) * 2 + c) * 4 + at
                    micro = at % 2 if turn == 0 else 1 - at % 2
                    target = ((y * 16 + 2 * place) * 2 + at // 2) * 4 + 2 * micro + c
                    route.append((source, target))
        got.append(lax.ppermute(picked[turn], ("y",) + PLANE + ("core", "x"), route))
    low = x // 2 == 0
    return jnp.concatenate(
        [jnp.where(low, got[0], got[1]), jnp.where(low, got[1], got[0])], axis=0
    )


def near(*arrays):
    return [pltpu.with_memory_space_constraint(array, pltpu.VMEM) for array in arrays]


def from_z(array, distance):
    return lax.ppermute(array, PLANE, [(j, (j - distance) % 16) for j in range(16)])


def from_x(array, distance):
    return lax.ppermute(array, "x", [(i, (i - distance) % 4) for i in range(4)])


def joined(*arrays):
    return jnp.concatenate(arrays, axis=0)


def on_device(clips, weights, cotangents):
    y, zh, zq, zp, core, x = (
        lax.axis_index(a) for a in ("y", "zh", "zq", "zp", "core", "x")
    )
    z = zh * 8 + zq * 2 + zp
    low = serves_low(y, z)
    layer = 2 * y + jnp.where(low, 0, 1)
    moved = low != (zh == 0)
    is_layer = [layer == l for l in range(LAYERS)]
    early = layer < 3
    first_core = core == 0
    even = zp == 0
    at = jnp.stack([core, x, z, jnp.where(low, 1, 0)]).astype(jnp.int32)

    x_hold = volume_half(clips, x, 0)
    carried = volume_half(cotangents, x, 3)
    own = lax.all_to_all(
        weights[0].transpose(1, 0, 2).reshape(27, 8, 2, 256), "core", split_axis=2, concat_axis=1
    ).reshape(27, 16, 256)
    own, x_hold, carried, at, is_layer, early, first_core, even, low, moved = (
        lax.optimization_barrier(
            (own, x_hold, carried, at, is_layer, early, first_core, even, low, moved)
        )
    )

    everywhere = pl.BlockSpec(memory_space=pltpu.VMEM)
    anywhere = pl.BlockSpec(memory_space=pl.ANY)
    scalar = pl.BlockSpec(memory_space=pltpu.SMEM)
    limits = pltpu.CompilerParams(vmem_limit_bytes=20 * 1024 * 1024)

    kernels = []
    for chunk in range(CHUNKS):
        part = own[None, EDGES[chunk] : EDGES[chunk + 1]]
        got = lax.ppermute(part, ("y",) + PLANE, EXCHANGE)
        part = jnp.where(moved, got, part)
        across, above, below = from_z(part, 8), from_z(part, 4), from_z(part, 12)
        nearer = from_z(joined(part, above), 2), from_z(joined(part, below), 14)
        part = joined(part, across, above, below, *nearer)
        before, after = from_x(part, 3), from_x(part, 1)
        far_low, far_high = from_x(before[:4], 3), from_x(after[4:], 1)
        kernels.append(
            pl.pallas_call(
                place_kernel,
                in_specs=[scalar] + [anywhere] * 5,
                out_shape=pltpu.VMEM((32,) + part.shape[1:], BF16),
                scratch_shapes=(pltpu.SemaphoreType.DMA((32,)),),
                compiler_params=limits,
                name="place_kernels",
            )(at, part, before, after, far_low, far_high)
        )

    tile = pltpu.VMEM((256, CELLS), BF16)
    forward = pl.pallas_call(
        forward_kernel,
        in_specs=[scalar] + [everywhere] * (2 + CHUNKS),
        out_shape=(tile, pltpu.VMEM((256, CELLS), F32), tile),
        scratch_shapes=(pltpu.VMEM((512, CELLS), F32),),
        compiler_params=limits,
        name="conv_forward",
    )
    backward = pl.pallas_call(
        backward_kernel,
        out_shape=(tile, tile),
        scratch_shapes=(pltpu.VMEM((3, 6, 6, 8, 512), F32),),
        compiler_params=limits,
        name="conv_backward",
    )
    places = ("y", "zp")

    skip = jnp.zeros((256, CELLS), BF16)
    for l in range(LAYERS):
        act, mine, other = forward(at, *near(x_hold, skip, *kernels))
        if l == LAYERS - 1:
            break
        both = lax.all_gather(other, "core", axis=0, tiled=False)
        update = mine + jnp.where(first_core, both[1], both[0]).astype(F32)
        out = (x_hold.astype(F32) + update).astype(BF16)
        if l == 3:
            skip = lax.ppermute(out, places, [(PLACE[j], PLACE[7 - j]) for j in range(4)])
            x_hold = jnp.where(is_layer[4], skip, x_hold)
        else:
            got = lax.ppermute(out, places, [(PLACE[l], PLACE[l + 1])])
            x_hold = jnp.where(is_layer[l + 1], got, x_hold)

    acts = act[None]
    gskip = jnp.zeros((256, CELLS), BF16)
    for l in reversed(range(LAYERS)):
        grad_low = (carried.astype(F32) + gskip.astype(F32)).astype(BF16)
        grads = lax.all_gather(grad_low, "core", axis=0, tiled=True)
        if l == 0:
            break
        sent, pre = backward(*near(grads, carried, gskip, x_hold, skip, *kernels))
        if l == 7:
            acts, sent = lax.optimization_barrier((acts, sent))
            above, below = from_z(acts, 4), from_z(acts, 12)
            across = from_z(acts, 8)
        elif l == 6:
            acts, across, above, below, sent = lax.optimization_barrier(
                (acts, across, above, below, sent)
            )
            nearer = from_z(joined(acts, above), 2), from_z(joined(acts, below), 14)
        elif l == 5:
            acts, sent = lax.optimization_barrier(
                (joined(acts, across, above, below, *nearer), sent)
            )
            before, after = from_x(acts, 3), from_x(acts, 1)
        elif l == 4:
            before, after, pre = lax.optimization_barrier((before, after, pre))
            far_low, far_high = from_x(before[:4], 3), from_x(after[4:], 1)
        elif l == 2:
            far_low, far_high, sent = lax.optimization_barrier((far_low, far_high, sent))
        if l == 4:
            whole = (sent.astype(F32) + pre.astype(F32)).astype(BF16)
            got = lax.ppermute(
                jnp.where(is_layer[4], whole, pre), places, [(PLACE[7 - j], PLACE[j]) for j in range(4)]
            )
            carried = jnp.where(is_layer[3], got, carried)
            gskip = jnp.where(early, got, gskip)
        else:
            got = lax.ppermute(sent, places, [(PLACE[l], PLACE[l - 1])])
            carried = jnp.where(is_layer[l - 1], got, carried)

    rows = grads.reshape(4, 8, 16, CELLS)

    def ordered(serves, parity):
        places_at = range(parity, 16, 2)
        if serves:
            order = [i if i < 8 else 15 - i for i in places_at]
        else:
            order = [i - 8 if i >= 8 else 7 - i for i in places_at]
        return jnp.stack([rows[:, i] for i in order], axis=1)

    rows = jnp.where(
        even,
        jnp.where(low, ordered(True, 0), ordered(False, 0)),
        jnp.where(low, ordered(True, 1), ordered(False, 1)),
    )
    rows = lax.all_to_all(rows, "x", split_axis=0, concat_axis=0)
    rows = lax.all_to_all(rows, ("zh", "zq"), split_axis=1, concat_axis=1).reshape(32, 16, CELLS)
    total = pl.pallas_call(
        weight_grad_kernel,
        in_specs=[scalar] + [everywhere] * 6,
        out_shape=pltpu.VMEM((432, 256), BF16),
        compiler_params=limits,
        name="weight_grad",
    )(at, rows, acts, before, after, far_low, far_high)
    total = lax.all_to_all(
        total.reshape(27, 2, 8, 256), "core", split_axis=1, concat_axis=1
    )
    got = lax.ppermute(total, ("y",) + PLANE, EXCHANGE)
    total = jnp.where(moved, got, total)
    return total.transpose(2, 0, 1, 3).reshape(1, 8, 27, 512).astype(F32)


def solution(mesh):
    fine = Mesh(
        mesh.devices.reshape(4, 2, 4, 2, 2, 4), ("y", "zh", "zq", "zp", "core", "x")
    )
    placed = (
        P(None, "x", ("zq", "zp", "core")),
        P(("y", "zh"), ("x", "zq", "zp", "core"), None, None),
        P(None, "x", ("zq", "zp", "core")),
    )
    return jax.shard_map(
        on_device,
        mesh=fine,
        in_specs=placed,
        out_specs=P(("y", "zh"), ("x", "zq", "zp", "core"), None, None),
        check_vma=False,
    )
```

```python
import jax
import jax.numpy as jnp
from jax import lax
from jax.experimental import pallas as pl
from jax.experimental.pallas import tpu as pltpu
from jax.sharding import Mesh, PartitionSpec as P

F32 = jnp.float32
BF16 = jnp.bfloat16
LAYERS = 8
CELLS = 128
TAPS = [(df, dh, dw) for df in (-1, 0, 1) for dh in (-1, 0, 1) for dw in (-1, 0, 1)]
PLACE = [2 * l if l < 4 else 15 - 2 * l for l in range(LAYERS)]
MIRRORED = (1, 3, 4, 6)
HOMES = [
    (l * 8 + z, PLACE[l] * 8 + (7 - z if l in MIRRORED else z)) for l in range(LAYERS) for z in range(8)
]
EDGES = (0, 6, 18, 27)
CHUNKS = len(EDGES) - 1
Z_ORDER = [0, 4, 2, 6, 1, 5, 3, 7]
X_ORDER = [0, 2, 1, 3]


def shifted(source, move):
    df, dh, dw = move
    if move == (0, 0, 0):
        return source
    lane = lax.broadcasted_iota(jnp.int32, (1, CELLS), 1)
    f, h, w = lane // 32 + df, (lane // 8) % 4 + dh, lane % 8 + dw
    inside = (f >= 0) & (f < 4) & (h >= 0) & (h < 4) & (w >= 0) & (w < 8)
    turned = pltpu.roll(source, (-(32 * df + 8 * dh + dw)) % CELLS, 1)
    return jnp.where(inside, turned, 0.0)


def tap_rows(kernels, k, blocks=slice(None)):
    chunk = max(c for c in range(CHUNKS) if EDGES[c] <= k)
    return kernels[chunk][blocks, k - EDGES[chunk]].reshape(-1, 256)


def carry_out(copies, sems):
    moves = [pltpu.make_async_copy(*copy, sems.at[n]) for n, copy in enumerate(copies)]
    for move in moves:
        move.start()
    for move in moves:
        move.wait()


def place_x_first(at_ref, gathered, out_ref, sems):
    x, z, flip = at_ref[1], at_ref[2], at_ref[3]
    copies = []
    for q, z_turn in enumerate(Z_ORDER):
        for r, x_turn in enumerate(X_ORDER):
            target = (x ^ x_turn) * 8 + (z ^ z_turn ^ flip)
            copies.append((gathered.at[q * 4 + r], out_ref.at[target]))
    carry_out(copies, sems)


def place_z_first(at_ref, own, before, after, far_low, far_high, out_ref, sems):
    x, z, flip = at_ref[1], at_ref[2], at_ref[3]
    copies = []
    for q, z_turn in enumerate(Z_ORDER):
        far = far_low.at[q] if q < 4 else far_high.at[q - 4]
        for turn, source in enumerate((own.at[q], after.at[q], far, before.at[q])):
            target = ((x + turn) % 4) * 8 + (z ^ z_turn ^ flip)
            copies.append((source, out_ref.at[target]))
    carry_out(copies, sems)


def forward_kernel(at_ref, x_ref, skip_ref, *refs):
    kernels, (act_ref, own_ref, other_ref) = refs[:CHUNKS], refs[CHUNKS:]
    core = at_ref[0]
    summed = x_ref[...].astype(F32) + skip_ref[...].astype(F32)
    act = (summed * jax.nn.sigmoid(summed)).astype(BF16)
    act_ref[...] = act
    act = act.astype(F32)
    groups = [range(first, first + 3) for first in range(0, 27, 3)]
    stacks = [
        jnp.concatenate([shifted(act, TAPS[k]).astype(BF16) for k in taps], axis=0)
        for taps in groups
    ]

    def rows(half):
        total = None
        for taps, stacked in zip(groups, stacks):
            matrix = [tap_rows(kernels, k, pl.ds(half * 16, 16)) for k in taps]
            part = lax.dot_general(
                jnp.concatenate(matrix, axis=1),
                stacked,
                (((1,), (0,)), ((), ())),
                preferred_element_type=F32,
            )
            total = part if total is None else total + part
        return total

    other_ref[...] = rows(1 - core).astype(BF16)
    own_ref[...] = rows(core)


def backward_kernel(g_ref, up_ref, gskip_ref, x_ref, skip_ref, *refs):
    kernels, (sent_ref, pre_ref, pad_ref) = refs[:CHUNKS], refs[CHUNKS:]
    grads = g_ref[...].astype(F32).T
    column = lax.broadcasted_iota(jnp.int32, (CELLS, 1), 0) % 8
    pad_ref[...] = jnp.zeros(pad_ref.shape, F32)
    for slot, move in enumerate((1, 0, -1)):
        turned = grads
        if move:
            turned = pltpu.roll(grads, (-move) % CELLS, 0)
            turned = jnp.where((column + move >= 0) & (column + move < 8), turned, 0.0)
        pad_ref[slot, 1:5, 1:5] = turned.reshape(4, 4, 8, 512)
    total = None
    for k, (df, dh, dw) in enumerate(TAPS):
        window = pad_ref[dw + 1, 1 - df : 5 - df, 1 - dh : 5 - dh]
        part = lax.dot_general(
            window.reshape(CELLS, 512).astype(BF16),
            tap_rows(kernels, k),
            (((1,), (0,)), ((), ())),
            preferred_element_type=F32,
        )
        total = part if total is None else total + part
    summed = x_ref[...].astype(F32) + skip_ref[...].astype(F32)
    sig = jax.nn.sigmoid(summed)
    pre = total.T * (sig * (1.0 + summed * (1.0 - sig)))
    pre_ref[...] = pre.astype(BF16)
    upstream = up_ref[...].astype(F32) + gskip_ref[...].astype(F32)
    sent_ref[...] = (upstream + pre).astype(BF16)


def weight_grad_kernel(at_ref, g_ref, own, before, after, far_low, far_high, out_ref):
    x, z = at_ref[1], at_ref[2]
    total = None
    for turn, piece in enumerate((own, after, None, before)):
        for q in range(0, 8, 2):
            left, right = [], []
            for place in (q, q + 1):
                row = ((x + turn) % 4) * 8 + (z ^ Z_ORDER[place])
                grads = g_ref[row].astype(F32)
                left.append(
                    jnp.concatenate(
                        [shifted(grads, tuple(-m for m in move)).astype(BF16) for move in TAPS],
                        axis=0,
                    )
                )
                if piece is not None:
                    right.append(piece[place])
                else:
                    right.append(far_low[place] if place < 4 else far_high[place - 4])
            part = lax.dot_general(
                jnp.concatenate(left, axis=1),
                jnp.concatenate(right, axis=1),
                (((1,), (1,)), ((), ())),
                preferred_element_type=F32,
            )
            total = part if total is None else total + part
    out_ref[...] = total.astype(BF16)


def volume_half(pair, x, section, mirrored):
    picked = [jnp.where(x % 2 == 0, pair[0], pair[1]), jnp.where(x % 2 == 0, pair[1], pair[0])]
    got = []
    for turn in range(2):
        route = []
        for z in range(8):
            for c in range(2):
                for at in range(4):
                    source = ((section * 8 + z) * 2 + c) * 4 + at
                    micro = at % 2 if turn == 0 else 1 - at % 2
                    to = section * 8 + (7 - z if mirrored else z)
                    route.append((source, (to * 2 + at // 2) * 4 + 2 * micro + c))
        got.append(lax.ppermute(picked[turn], ("y", "zh", "zl", "core", "x"), route))
    low = x // 2 == 0
    return jnp.concatenate(
        [jnp.where(low, got[0], got[1]), jnp.where(low, got[1], got[0])], axis=0
    )


def near(*arrays):
    return [pltpu.with_memory_space_constraint(array, pltpu.VMEM) for array in arrays]


def with_z(array, bit):
    other = lax.ppermute(array, "zl", [(i, i ^ bit) for i in range(8)])
    return jnp.concatenate([array, other], axis=0)


def with_x(array, bit):
    other = lax.ppermute(array, "x", [(i, i ^ bit) for i in range(4)])
    return jnp.concatenate([array, other], axis=0)


def from_x(array, distance):
    return lax.ppermute(array, "x", [(i, (i - distance) % 4) for i in range(4)])


def on_device(clips, weights, cotangents):
    y, zh, z, core, x = (lax.axis_index(a) for a in ("y", "zh", "zl", "core", "x"))
    layer = jnp.where(zh == 0, y, 7 - y)
    is_layer = [layer == l for l in range(LAYERS)]
    mirrored = is_layer[1] | is_layer[3] | is_layer[4] | is_layer[6]
    early = layer < 3
    first_core = core == 0
    at = jnp.stack([core, x, z, jnp.where(mirrored, 7, 0)]).astype(jnp.int32)
    section = ("y", "zh")

    x_hold = volume_half(clips, x, PLACE[0], False)
    own = lax.all_to_all(
        weights[0].transpose(1, 0, 2).reshape(27, 8, 2, 256), "core", split_axis=2, concat_axis=1
    ).reshape(27, 16, 256)
    own = lax.ppermute(own, section + ("zl",), HOMES)
    own, x_hold, at, is_layer, early, first_core, mirrored = lax.optimization_barrier(
        (own, x_hold, at, is_layer, early, first_core, mirrored)
    )

    everywhere = pl.BlockSpec(memory_space=pltpu.VMEM)
    anywhere = pl.BlockSpec(memory_space=pl.ANY)
    scalar = pl.BlockSpec(memory_space=pltpu.SMEM)
    limits = pltpu.CompilerParams(vmem_limit_bytes=20 * 1024 * 1024)

    def place(kernel, *pieces):
        taps = pieces[0].shape[1]
        return pl.pallas_call(
            kernel,
            in_specs=[scalar] + [anywhere] * len(pieces),
            out_shape=pltpu.VMEM((32, taps, 16, 256), BF16),
            scratch_shapes=(pltpu.SemaphoreType.DMA((32,)),),
            compiler_params=limits,
            name="place_kernels",
        )(at, *pieces)

    parts = [own[None, EDGES[c] : EDGES[c + 1]] for c in range(CHUNKS)]
    parts[0] = with_x(with_x(parts[0], 2), 1)
    for bit in (4, 2, 1):
        for c in range(1, CHUNKS):
            parts[c] = with_z(parts[c], bit)
    kernels = [None]
    for part in parts[1:]:
        before, after = from_x(part, 3), from_x(part, 1)
        far_low, far_high = from_x(before[:4], 3), from_x(after[4:], 1)
        kernels.append(place(place_z_first, part, before, after, far_low, far_high))
    for bit in (4, 2, 1):
        parts[0] = with_z(parts[0], bit)
    kernels[0] = place(place_x_first, parts[0])

    tile = pltpu.VMEM((256, CELLS), BF16)
    forward = pl.pallas_call(
        forward_kernel,
        in_specs=[scalar] + [everywhere] * (2 + CHUNKS),
        out_shape=(tile, pltpu.VMEM((256, CELLS), F32), tile),
        compiler_params=limits,
        name="conv_forward",
    )
    backward = pl.pallas_call(
        backward_kernel,
        out_shape=(tile, tile),
        scratch_shapes=(pltpu.VMEM((3, 6, 6, 8, 512), F32),),
        compiler_params=limits,
        name="conv_backward",
    )
    across = [(i, 15 - i) for i in range(8)]

    skip = jnp.zeros((256, CELLS), BF16)
    for l in range(LAYERS):
        act, mine, other = forward(at, *near(x_hold, skip, *kernels))
        if l == LAYERS - 1:
            break
        both = lax.all_gather(other, "core", axis=0, tiled=False)
        update = mine + jnp.where(first_core, both[1], both[0]).astype(F32)
        out = (x_hold.astype(F32) + update).astype(BF16)
        if l == 0:
            cotangents, out = lax.optimization_barrier((cotangents, out))
            carried = volume_half(cotangents, x, PLACE[7], True)
        elif l == 2:
            carried, out = lax.optimization_barrier((carried, out))
        if l == 3:
            skip = lax.ppermute(out, ("zh", "zl"), across)
            x_hold = jnp.where(is_layer[4], skip, x_hold)
        else:
            got = lax.ppermute(out, section, [(PLACE[l], PLACE[l + 1])])
            x_hold = jnp.where(is_layer[l + 1], got, x_hold)

    acts = act[None]
    gskip = jnp.zeros((256, CELLS), BF16)
    for l in reversed(range(LAYERS)):
        grad_low = (carried.astype(F32) + gskip.astype(F32)).astype(BF16)
        grads = lax.all_gather(grad_low, "core", axis=0, tiled=True)
        if l == 0:
            break
        sent, pre = backward(*near(grads, carried, gskip, x_hold, skip, *kernels))
        if l > 4:
            acts, sent = lax.optimization_barrier((acts, sent))
            acts = with_z(acts, 1 << (l - 5))
        elif l == 4:
            acts, sent = lax.optimization_barrier((acts, sent))
            before, after = from_x(acts, 3), from_x(acts, 1)
        elif l == 3:
            before, after, sent = lax.optimization_barrier((before, after, sent))
            far_low, far_high = from_x(before[:4], 3), from_x(after[4:], 1)
        elif l == 2:
            far_low, far_high, sent = lax.optimization_barrier((far_low, far_high, sent))
        if l == 4:
            whole = (sent.astype(F32) + pre.astype(F32)).astype(BF16)
            got = lax.ppermute(
                jnp.where(is_layer[4], whole, pre), ("zh", "zl"), [(b, a) for a, b in across]
            )
            carried = jnp.where(is_layer[3], got, carried)
            gskip = jnp.where(early, got, gskip)
        else:
            got = lax.ppermute(sent, section, [(PLACE[l], PLACE[l - 1])])
            carried = jnp.where(is_layer[l - 1], got, carried)

    rows = grads.reshape(4, 8, 16, CELLS)

    rows = jnp.where(mirrored, rows[:, ::-1], rows)
    rows = lax.all_to_all(rows, "x", split_axis=0, concat_axis=0)
    rows = lax.all_to_all(rows, "zl", split_axis=1, concat_axis=1).reshape(32, 16, CELLS)
    total = pl.pallas_call(
        weight_grad_kernel,
        in_specs=[scalar] + [everywhere] * 6,
        out_shape=pltpu.VMEM((432, 256), BF16),
        compiler_params=limits,
        name="weight_grad",
    )(at, rows, acts, before, after, far_low, far_high)
    total = lax.all_to_all(
        total.reshape(27, 2, 8, 256), "core", split_axis=1, concat_axis=1
    )
    total = lax.ppermute(total, section + ("zl",), [(b, a) for a, b in HOMES])
    return total.transpose(2, 0, 1, 3).reshape(1, 8, 27, 512).astype(F32)


def solution(mesh):
    fine = Mesh(mesh.devices.reshape(4, 2, 8, 2, 4), ("y", "zh", "zl", "core", "x"))
    placed = (
        P(None, "x", ("zl", "core")),
        P(("y", "zh"), ("x", "zl", "core"), None, None),
        P(None, "x", ("zl", "core")),
    )
    return jax.shard_map(
        on_device,
        mesh=fine,
        in_specs=placed,
        out_specs=P(("y", "zh"), ("x", "zl", "core"), None, None),
        check_vma=False,
    )
```

```python
import jax
import jax.numpy as jnp
from jax import lax
from jax.experimental import pallas as pl
from jax.experimental.pallas import tpu as pltpu
from jax.sharding import Mesh, PartitionSpec as P

F32 = jnp.float32
BF16 = jnp.bfloat16
LAYERS = 8
CELLS = 128
TAPS = [(df, dh, dw) for df in (-1, 0, 1) for dh in (-1, 0, 1) for dw in (-1, 0, 1)]
PLACE = [2 * l if l < 4 else 15 - 2 * l for l in range(LAYERS)]
MIRRORED = (1, 3, 4, 6)
HOMES = [
    (l * 8 + z, PLACE[l] * 8 + (7 - z if l in MIRRORED else z)) for l in range(LAYERS) for z in range(8)
]
EDGES = (0, 6, 18, 27)
CHUNKS = len(EDGES) - 1
Z_ORDER = [0, 4, 2, 6, 1, 5, 3, 7]
X_ORDER = [0, 2, 1, 3]


def shifted(source, move):
    df, dh, dw = move
    if move == (0, 0, 0):
        return source
    lane = lax.broadcasted_iota(jnp.int32, (1, CELLS), 1)
    f, h, w = lane // 32 + df, (lane // 8) % 4 + dh, lane % 8 + dw
    inside = (f >= 0) & (f < 4) & (h >= 0) & (h < 4) & (w >= 0) & (w < 8)
    turned = pltpu.roll(source, (-(32 * df + 8 * dh + dw)) % CELLS, 1)
    return jnp.where(inside, turned, 0.0)


def tap_rows(kernels, k, blocks=slice(None)):
    chunk = max(c for c in range(CHUNKS) if EDGES[c] <= k)
    return kernels[chunk][blocks, k - EDGES[chunk]].reshape(-1, 256)


def mirror_bits():
    return 7 * (lax.axis_index("y") % 2)


def carry_out(copies, sems):
    moves = [pltpu.make_async_copy(*copy, sems.at[n]) for n, copy in enumerate(copies)]
    for move in moves:
        move.start()
    for move in moves:
        move.wait()


def place_x_first(gathered, out_ref, sems):
    x, z, flip = lax.axis_index("x"), lax.axis_index("zl"), mirror_bits()
    copies = []
    for q, z_turn in enumerate(Z_ORDER):
        for r, x_turn in enumerate(X_ORDER):
            target = (x ^ x_turn) * 8 + (z ^ z_turn ^ flip)
            copies.append((gathered.at[q * 4 + r], out_ref.at[target]))
    carry_out(copies, sems)


def place_z_first(own, before, after, far_low, far_high, out_ref, sems):
    x, z, flip = lax.axis_index("x"), lax.axis_index("zl"), mirror_bits()
    copies = []
    for q, z_turn in enumerate(Z_ORDER):
        far = far_low.at[q] if q < 4 else far_high.at[q - 4]
        for turn, source in enumerate((own.at[q], after.at[q], far, before.at[q])):
            target = ((x + turn) % 4) * 8 + (z ^ z_turn ^ flip)
            copies.append((source, out_ref.at[target]))
    carry_out(copies, sems)


def forward_kernel(x_ref, skip_ref, *refs):
    kernels, (act_ref, own_ref, other_ref) = refs[:CHUNKS], refs[CHUNKS:]
    core = lax.axis_index("core")
    summed = x_ref[...].astype(F32) + skip_ref[...].astype(F32)
    act = (summed * jax.nn.sigmoid(summed)).astype(BF16)
    act_ref[...] = act
    act = act.astype(F32)
    groups = [range(first, first + 3) for first in range(0, 27, 3)]
    stacks = [
        jnp.concatenate([shifted(act, TAPS[k]).astype(BF16) for k in taps], axis=0)
        for taps in groups
    ]

    def rows(half):
        total = None
        for taps, stacked in zip(groups, stacks):
            matrix = [tap_rows(kernels, k, pl.ds(half * 16, 16)) for k in taps]
            part = lax.dot_general(
                jnp.concatenate(matrix, axis=1),
                stacked,
                (((1,), (0,)), ((), ())),
                preferred_element_type=F32,
            )
            total = part if total is None else total + part
        return total

    other_ref[...] = rows(1 - core).astype(BF16)
    own_ref[...] = rows(core)


def backward_kernel(g_ref, up_ref, gskip_ref, x_ref, skip_ref, *refs):
    kernels, (sent_ref, pre_ref, pad_ref) = refs[:CHUNKS], refs[CHUNKS:]
    grads = g_ref[...].astype(F32).T
    column = lax.broadcasted_iota(jnp.int32, (CELLS, 1), 0) % 8
    pad_ref[...] = jnp.zeros(pad_ref.shape, F32)
    for slot, move in enumerate((1, 0, -1)):
        turned = grads
        if move:
            turned = pltpu.roll(grads, (-move) % CELLS, 0)
            turned = jnp.where((column + move >= 0) & (column + move < 8), turned, 0.0)
        pad_ref[slot, 1:5, 1:5] = turned.reshape(4, 4, 8, 512)
    total = None
    for k, (df, dh, dw) in enumerate(TAPS):
        window = pad_ref[dw + 1, 1 - df : 5 - df, 1 - dh : 5 - dh]
        part = lax.dot_general(
            window.reshape(CELLS, 512).astype(BF16),
            tap_rows(kernels, k),
            (((1,), (0,)), ((), ())),
            preferred_element_type=F32,
        )
        total = part if total is None else total + part
    summed = x_ref[...].astype(F32) + skip_ref[...].astype(F32)
    sig = jax.nn.sigmoid(summed)
    pre = total.T * (sig * (1.0 + summed * (1.0 - sig)))
    pre_ref[...] = pre.astype(BF16)
    upstream = up_ref[...].astype(F32) + gskip_ref[...].astype(F32)
    sent_ref[...] = (upstream + pre).astype(BF16)


def weight_grad_kernel(g_ref, own, before, after, far_low, far_high, out_ref):
    x, z = lax.axis_index("x"), lax.axis_index("zl")
    total = None
    for turn, piece in enumerate((own, after, None, before)):
        for q in range(0, 8, 2):
            left, right = [], []
            for place in (q, q + 1):
                row = ((x + turn) % 4) * 8 + (z ^ Z_ORDER[place])
                grads = g_ref[row].astype(F32)
                left.append(
                    jnp.concatenate(
                        [shifted(grads, tuple(-m for m in move)).astype(BF16) for move in TAPS],
                        axis=0,
                    )
                )
                if piece is not None:
                    right.append(piece[place])
                else:
                    right.append(far_low[place] if place < 4 else far_high[place - 4])
            part = lax.dot_general(
                jnp.concatenate(left, axis=1),
                jnp.concatenate(right, axis=1),
                (((1,), (1,)), ((), ())),
                preferred_element_type=F32,
            )
            total = part if total is None else total + part
    out_ref[...] = total.astype(BF16)


def volume_half(pair, x, section, mirrored):
    picked = [jnp.where(x % 2 == 0, pair[0], pair[1]), jnp.where(x % 2 == 0, pair[1], pair[0])]
    got = []
    for turn in range(2):
        route = []
        for z in range(8):
            for c in range(2):
                for at in range(4):
                    source = ((section * 8 + z) * 2 + c) * 4 + at
                    micro = at % 2 if turn == 0 else 1 - at % 2
                    to = section * 8 + (7 - z if mirrored else z)
                    route.append((source, (to * 2 + at // 2) * 4 + 2 * micro + c))
        got.append(lax.ppermute(picked[turn], ("y", "zh", "zl", "core", "x"), route))
    low = x // 2 == 0
    return jnp.concatenate(
        [jnp.where(low, got[0], got[1]), jnp.where(low, got[1], got[0])], axis=0
    )


def near(*arrays):
    return [pltpu.with_memory_space_constraint(array, pltpu.VMEM) for array in arrays]


def with_z(array, bit):
    other = lax.ppermute(array, "zl", [(i, i ^ bit) for i in range(8)])
    return jnp.concatenate([array, other], axis=0)


def with_x(array, bit):
    other = lax.ppermute(array, "x", [(i, i ^ bit) for i in range(4)])
    return jnp.concatenate([array, other], axis=0)


def from_x(array, distance):
    return lax.ppermute(array, "x", [(i, (i - distance) % 4) for i in range(4)])


def on_device(clips, weights, cotangents):
    y, zh, core, x = (lax.axis_index(a) for a in ("y", "zh", "core", "x"))
    layer = jnp.where(zh == 0, y, 7 - y)
    is_layer = [layer == l for l in range(LAYERS)]
    early = layer < 3
    first_core = core == 0
    section = ("y", "zh")

    x_hold = volume_half(clips, x, PLACE[0], False)
    own = lax.all_to_all(
        weights[0].transpose(1, 0, 2).reshape(27, 8, 2, 256), "core", split_axis=2, concat_axis=1
    ).reshape(27, 16, 256)
    own = lax.ppermute(own, section + ("zl",), HOMES)
    own, x_hold, is_layer, early, first_core = lax.optimization_barrier(
        (own, x_hold, is_layer, early, first_core)
    )

    everywhere = pl.BlockSpec(memory_space=pltpu.VMEM)
    anywhere = pl.BlockSpec(memory_space=pl.ANY)
    limits = pltpu.CompilerParams(vmem_limit_bytes=20 * 1024 * 1024)

    def place(kernel, *pieces):
        taps = pieces[0].shape[1]
        return pl.pallas_call(
            kernel,
            in_specs=[anywhere] * len(pieces),
            out_shape=pltpu.VMEM((32, taps, 16, 256), BF16),
            scratch_shapes=(pltpu.SemaphoreType.DMA((32,)),),
            compiler_params=limits,
            name="place_kernels",
        )(*pieces)

    parts = [own[None, EDGES[c] : EDGES[c + 1]] for c in range(CHUNKS)]
    parts[0] = with_x(with_x(parts[0], 2), 1)
    for bit in (4, 2, 1):
        for c in range(1, CHUNKS):
            parts[c] = with_z(parts[c], bit)
    kernels = [None]
    for part in parts[1:]:
        before, after = from_x(part, 3), from_x(part, 1)
        far_low, far_high = from_x(before[:4], 3), from_x(after[4:], 1)
        kernels.append(place(place_z_first, part, before, after, far_low, far_high))
    for bit in (4, 2, 1):
        parts[0] = with_z(parts[0], bit)
    kernels[0] = place(place_x_first, parts[0])

    tile = pltpu.VMEM((256, CELLS), BF16)
    forward = pl.pallas_call(
        forward_kernel,
        in_specs=[everywhere] * (2 + CHUNKS),
        out_shape=(tile, pltpu.VMEM((256, CELLS), F32), tile),
        compiler_params=limits,
        name="conv_forward",
    )
    backward = pl.pallas_call(
        backward_kernel,
        out_shape=(tile, tile),
        scratch_shapes=(pltpu.VMEM((3, 6, 6, 8, 512), F32),),
        compiler_params=limits,
        name="conv_backward",
    )
    across = [(i, 15 - i) for i in range(8)]

    skip = jnp.zeros((256, CELLS), BF16)
    for l in range(LAYERS):
        act, mine, other = forward(*near(x_hold, skip, *kernels))
        if l == LAYERS - 1:
            break
        both = lax.all_gather(other, "core", axis=0, tiled=False)
        update = mine + jnp.where(first_core, both[1], both[0]).astype(F32)
        out = (x_hold.astype(F32) + update).astype(BF16)
        if l == 0:
            cotangents, out = lax.optimization_barrier((cotangents, out))
            carried = volume_half(cotangents, x, PLACE[7], True)
        elif l == 2:
            carried, out = lax.optimization_barrier((carried, out))
        if l == 3:
            skip = lax.ppermute(out, ("zh", "zl"), across)
            x_hold = jnp.where(is_layer[4], skip, x_hold)
        else:
            got = lax.ppermute(out, section, [(PLACE[l], PLACE[l + 1])])
            x_hold = jnp.where(is_layer[l + 1], got, x_hold)

    acts = act[None]
    to_home = [(b, a) for a, b in HOMES]
    gskip = jnp.zeros((256, CELLS), BF16)
    for l in reversed(range(LAYERS)):
        grad_low = (carried.astype(F32) + gskip.astype(F32)).astype(BF16)
        if l == 0:
            grad_low = lax.ppermute(grad_low, section + ("zl",), to_home)
        grads = lax.all_gather(grad_low, "core", axis=0, tiled=True)
        if l == 0:
            break
        sent, pre = backward(*near(grads, carried, gskip, x_hold, skip, *kernels))
        if l == 7:
            acts, sent = lax.optimization_barrier((acts, sent))
            acts = lax.ppermute(acts, section + ("zl",), to_home)
        elif l > 3:
            acts, sent = lax.optimization_barrier((acts, sent))
            acts = with_z(acts, 1 << (l - 4))
        elif l == 3:
            acts, sent = lax.optimization_barrier((acts, sent))
            before, after = from_x(acts, 3), from_x(acts, 1)
        elif l == 2:
            before, after, sent = lax.optimization_barrier((before, after, sent))
            far_low, far_high = from_x(before[:4], 3), from_x(after[4:], 1)
        else:
            far_low, far_high, sent = lax.optimization_barrier((far_low, far_high, sent))
        if l == 4:
            whole = (sent.astype(F32) + pre.astype(F32)).astype(BF16)
            got = lax.ppermute(
                jnp.where(is_layer[4], whole, pre), ("zh", "zl"), [(b, a) for a, b in across]
            )
            carried = jnp.where(is_layer[3], got, carried)
            gskip = jnp.where(early, got, gskip)
        else:
            got = lax.ppermute(sent, section, [(PLACE[l], PLACE[l - 1])])
            carried = jnp.where(is_layer[l - 1], got, carried)

    rows = grads.reshape(4, 8, 16, CELLS)

    rows = lax.all_to_all(rows, "x", split_axis=0, concat_axis=0)
    rows = lax.all_to_all(rows, "zl", split_axis=1, concat_axis=1).reshape(32, 16, CELLS)
    total = pl.pallas_call(
        weight_grad_kernel,
        in_specs=[everywhere] * 6,
        out_shape=pltpu.VMEM((432, 256), BF16),
        compiler_params=limits,
        name="weight_grad",
    )(rows, acts, before, after, far_low, far_high)
    total = lax.all_to_all(
        total.reshape(27, 2, 8, 256), "core", split_axis=1, concat_axis=1
    )
    return total.transpose(2, 0, 1, 3).reshape(1, 8, 27, 512).astype(F32)


def solution(mesh):
    fine = Mesh(mesh.devices.reshape(4, 2, 8, 2, 4), ("y", "zh", "zl", "core", "x"))
    placed = (
        P(None, "x", ("zl", "core")),
        P(("y", "zh"), ("x", "zl", "core"), None, None),
        P(None, "x", ("zl", "core")),
    )
    return jax.shard_map(
        on_device,
        mesh=fine,
        in_specs=placed,
        out_specs=P(("y", "zh"), ("x", "zl", "core"), None, None),
        check_vma=False,
    )
```

```python
import jax
import jax.numpy as jnp
from jax import lax
from jax.experimental import pallas as pl
from jax.experimental.pallas import tpu as pltpu
from jax.sharding import Mesh, PartitionSpec as P

F32 = jnp.float32
BF16 = jnp.bfloat16
LAYERS = 8
CELLS = 128
TAPS = [(df, dh, dw) for df in (-1, 0, 1) for dh in (-1, 0, 1) for dw in (-1, 0, 1)]
PLACE = [0, 1, 3, 5, 4, 2, 6, 7]


def between(source, target):
    crossing = source % 2 != target % 2
    return [(source * 8 + z, target * 8 + (7 - z if crossing else z)) for z in range(8)]


HOMES = [pair for l in range(LAYERS) for pair in between(l, PLACE[l])]
SKIPS = [pair for l in range(LAYERS // 2) for pair in between(PLACE[l], PLACE[7 - l])]
EDGES = (0, 6, 18, 27)
CHUNKS = len(EDGES) - 1
Z_ORDER = [0, 4, 2, 6, 1, 5, 3, 7]
X_ORDER = [0, 2, 1, 3]


def shifted(source, move):
    df, dh, dw = move
    if move == (0, 0, 0):
        return source
    lane = lax.broadcasted_iota(jnp.int32, (1, CELLS), 1)
    f, h, w = lane // 32 + df, (lane // 8) % 4 + dh, lane % 8 + dw
    inside = (f >= 0) & (f < 4) & (h >= 0) & (h < 4) & (w >= 0) & (w < 8)
    turned = pltpu.roll(source, (-(32 * df + 8 * dh + dw)) % CELLS, 1)
    return jnp.where(inside, turned, 0.0)


def tap_rows(kernels, k, blocks=slice(None)):
    chunk = max(c for c in range(CHUNKS) if EDGES[c] <= k)
    return kernels[chunk][blocks, k - EDGES[chunk]].reshape(-1, 256)


def mirror_bits():
    return jnp.where(lax.axis_index("y") == 1, 7, 0)


def carry_out(copies, sems):
    moves = [pltpu.make_async_copy(*copy, sems.at[n]) for n, copy in enumerate(copies)]
    for move in moves:
        move.start()
    for move in moves:
        move.wait()


def place_x_first(gathered, out_ref, sems):
    x, z, flip = lax.axis_index("x"), lax.axis_index("zl"), mirror_bits()
    copies = []
    for q, z_turn in enumerate(Z_ORDER):
        for r, x_turn in enumerate(X_ORDER):
            target = (x ^ x_turn) * 8 + (z ^ z_turn ^ flip)
            copies.append((gathered.at[q * 4 + r], out_ref.at[target]))
    carry_out(copies, sems)


def place_z_first(own, before, after, far_low, far_high, out_ref, sems):
    x, z, flip = lax.axis_index("x"), lax.axis_index("zl"), mirror_bits()
    copies = []
    for q, z_turn in enumerate(Z_ORDER):
        far = far_low.at[q] if q < 4 else far_high.at[q - 4]
        for turn, source in enumerate((own.at[q], after.at[q], far, before.at[q])):
            target = ((x + turn) % 4) * 8 + (z ^ z_turn ^ flip)
            copies.append((source, out_ref.at[target]))
    carry_out(copies, sems)


def forward_kernel(x_ref, skip_ref, *refs):
    kernels, (act_ref, own_ref, other_ref) = refs[:CHUNKS], refs[CHUNKS:]
    core = lax.axis_index("core")
    summed = x_ref[...].astype(F32) + skip_ref[...].astype(F32)
    act = (summed * jax.nn.sigmoid(summed)).astype(BF16)
    act_ref[...] = act
    act = act.astype(F32)
    groups = [range(first, first + 3) for first in range(0, 27, 3)]
    stacks = [
        jnp.concatenate([shifted(act, TAPS[k]).astype(BF16) for k in taps], axis=0)
        for taps in groups
    ]

    def rows(half):
        total = None
        for taps, stacked in zip(groups, stacks):
            matrix = [tap_rows(kernels, k, pl.ds(half * 16, 16)) for k in taps]
            part = lax.dot_general(
                jnp.concatenate(matrix, axis=1),
                stacked,
                (((1,), (0,)), ((), ())),
                preferred_element_type=F32,
            )
            total = part if total is None else total + part
        return total

    other_ref[...] = rows(1 - core).astype(BF16)
    own_ref[...] = rows(core)


def backward_kernel(g_ref, up_ref, gskip_ref, x_ref, skip_ref, *refs):
    kernels, (sent_ref, pre_ref, pad_ref) = refs[:CHUNKS], refs[CHUNKS:]
    grads = g_ref[...].astype(F32).T
    column = lax.broadcasted_iota(jnp.int32, (CELLS, 1), 0) % 8
    pad_ref[...] = jnp.zeros(pad_ref.shape, F32)
    for slot, move in enumerate((1, 0, -1)):
        turned = grads
        if move:
            turned = pltpu.roll(grads, (-move) % CELLS, 0)
            turned = jnp.where((column + move >= 0) & (column + move < 8), turned, 0.0)
        pad_ref[slot, 1:5, 1:5] = turned.reshape(4, 4, 8, 512)
    total = None
    for k, (df, dh, dw) in enumerate(TAPS):
        window = pad_ref[dw + 1, 1 - df : 5 - df, 1 - dh : 5 - dh]
        part = lax.dot_general(
            window.reshape(CELLS, 512).astype(BF16),
            tap_rows(kernels, k),
            (((1,), (0,)), ((), ())),
            preferred_element_type=F32,
        )
        total = part if total is None else total + part
    summed = x_ref[...].astype(F32) + skip_ref[...].astype(F32)
    sig = jax.nn.sigmoid(summed)
    pre = total.T * (sig * (1.0 + summed * (1.0 - sig)))
    pre_ref[...] = pre.astype(BF16)
    upstream = up_ref[...].astype(F32) + gskip_ref[...].astype(F32)
    sent_ref[...] = (upstream + pre).astype(BF16)


def weight_grad_kernel(g_ref, own, before, after, far_low, far_high, out_ref):
    x, z = lax.axis_index("x"), lax.axis_index("zl")
    total = None
    for turn, piece in enumerate((own, after, None, before)):
        for q in range(0, 8, 2):
            left, right = [], []
            for place in (q, q + 1):
                row = ((x + turn) % 4) * 8 + (z ^ Z_ORDER[place])
                grads = g_ref[row].astype(F32)
                left.append(
                    jnp.concatenate(
                        [shifted(grads, tuple(-m for m in move)).astype(BF16) for move in TAPS],
                        axis=0,
                    )
                )
                if piece is not None:
                    right.append(piece[place])
                else:
                    right.append(far_low[place] if place < 4 else far_high[place - 4])
            part = lax.dot_general(
                jnp.concatenate(left, axis=1),
                jnp.concatenate(right, axis=1),
                (((1,), (1,)), ((), ())),
                preferred_element_type=F32,
            )
            total = part if total is None else total + part
    out_ref[...] = total.astype(BF16)


def volume_half(pair, x, section, mirrored):
    picked = [jnp.where(x % 2 == 0, pair[0], pair[1]), jnp.where(x % 2 == 0, pair[1], pair[0])]
    got = []
    for turn in range(2):
        route = []
        for z in range(8):
            for c in range(2):
                for at in range(4):
                    source = ((section * 8 + z) * 2 + c) * 4 + at
                    micro = at % 2 if turn == 0 else 1 - at % 2
                    to = section * 8 + (7 - z if mirrored else z)
                    route.append((source, (to * 2 + at // 2) * 4 + 2 * micro + c))
        got.append(lax.ppermute(picked[turn], ("y", "zh", "zl", "core", "x"), route))
    low = x // 2 == 0
    return jnp.concatenate(
        [jnp.where(low, got[0], got[1]), jnp.where(low, got[1], got[0])], axis=0
    )


def near(*arrays):
    return [pltpu.with_memory_space_constraint(array, pltpu.VMEM) for array in arrays]


def with_z(array, bit):
    other = lax.ppermute(array, "zl", [(i, i ^ bit) for i in range(8)])
    return jnp.concatenate([array, other], axis=0)


def with_x(array, bit):
    other = lax.ppermute(array, "x", [(i, i ^ bit) for i in range(4)])
    return jnp.concatenate([array, other], axis=0)


def from_x(array, distance):
    return lax.ppermute(array, "x", [(i, (i - distance) % 4) for i in range(4)])


def on_device(clips, weights, cotangents):
    y, zh, core, x = (lax.axis_index(a) for a in ("y", "zh", "core", "x"))
    is_layer = [2 * y + zh == PLACE[l] for l in range(LAYERS)]
    early = is_layer[0] | is_layer[1] | is_layer[2]
    first_core = core == 0
    chips = ("y", "zh", "zl")

    x_hold = volume_half(clips, x, PLACE[0], False)
    own = lax.all_to_all(
        weights[0].transpose(1, 0, 2).reshape(27, 8, 2, 256), "core", split_axis=2, concat_axis=1
    ).reshape(27, 16, 256)
    own = lax.ppermute(own, chips, HOMES)
    own, x_hold, is_layer, early, first_core = lax.optimization_barrier(
        (own, x_hold, is_layer, early, first_core)
    )

    everywhere = pl.BlockSpec(memory_space=pltpu.VMEM)
    anywhere = pl.BlockSpec(memory_space=pl.ANY)
    limits = pltpu.CompilerParams(vmem_limit_bytes=20 * 1024 * 1024)

    def place(kernel, *pieces):
        taps = pieces[0].shape[1]
        return pl.pallas_call(
            kernel,
            in_specs=[anywhere] * len(pieces),
            out_shape=pltpu.VMEM((32, taps, 16, 256), BF16),
            scratch_shapes=(pltpu.SemaphoreType.DMA((32,)),),
            compiler_params=limits,
            name="place_kernels",
        )(*pieces)

    parts = [own[None, EDGES[c] : EDGES[c + 1]] for c in range(CHUNKS)]
    parts[0] = with_x(with_x(parts[0], 2), 1)
    for bit in (4, 2, 1):
        for c in range(1, CHUNKS):
            parts[c] = with_z(parts[c], bit)
    kernels = [None]
    for part in parts[1:]:
        before, after = from_x(part, 3), from_x(part, 1)
        far_low, far_high = from_x(before[:4], 3), from_x(after[4:], 1)
        kernels.append(place(place_z_first, part, before, after, far_low, far_high))
    for bit in (4, 2, 1):
        parts[0] = with_z(parts[0], bit)
    kernels[0] = place(place_x_first, parts[0])

    tile = pltpu.VMEM((256, CELLS), BF16)
    forward = pl.pallas_call(
        forward_kernel,
        in_specs=[everywhere] * (2 + CHUNKS),
        out_shape=(tile, pltpu.VMEM((256, CELLS), F32), tile),
        compiler_params=limits,
        name="conv_forward",
    )
    backward = pl.pallas_call(
        backward_kernel,
        out_shape=(tile, tile),
        scratch_shapes=(pltpu.VMEM((3, 6, 6, 8, 512), F32),),
        compiler_params=limits,
        name="conv_backward",
    )

    skip = jnp.zeros((256, CELLS), BF16)
    for l in range(LAYERS):
        act, mine, other = forward(*near(x_hold, skip, *kernels))
        if l == LAYERS - 1:
            break
        both = lax.all_gather(other, "core", axis=0, tiled=False)
        update = mine + jnp.where(first_core, both[1], both[0]).astype(F32)
        out = (x_hold.astype(F32) + update).astype(BF16)
        if l == 0:
            cotangents, out = lax.optimization_barrier((cotangents, out))
            carried = volume_half(cotangents, x, PLACE[7], True)
        elif l == 2:
            carried, out = lax.optimization_barrier((carried, out))
        if l == 3:
            skip = lax.ppermute(out, chips, SKIPS)
            x_hold = jnp.where(is_layer[4], skip, x_hold)
        else:
            got = lax.ppermute(out, chips, between(PLACE[l], PLACE[l + 1]))
            x_hold = jnp.where(is_layer[l + 1], got, x_hold)

    acts = act[None]
    to_home = [(b, a) for a, b in HOMES]
    gskip = jnp.zeros((256, CELLS), BF16)
    for l in reversed(range(LAYERS)):
        grad_low = (carried.astype(F32) + gskip.astype(F32)).astype(BF16)
        if l == 0:
            grad_low = lax.ppermute(grad_low, chips, to_home)
            break
        grads = lax.all_gather(grad_low, "core", axis=0, tiled=True)
        sent, pre = backward(*near(grads, carried, gskip, x_hold, skip, *kernels))
        if l == 7:
            acts, sent = lax.optimization_barrier((acts, sent))
            acts = lax.ppermute(acts, chips, to_home)
        elif l > 3:
            acts, sent = lax.optimization_barrier((acts, sent))
            acts = with_z(acts, 1 << (l - 4))
        elif l == 3:
            acts, sent = lax.optimization_barrier((acts, sent))
            before, after = from_x(acts, 3), from_x(acts, 1)
        elif l == 2:
            before, after, sent = lax.optimization_barrier((before, after, sent))
            far_low, far_high = from_x(before[:4], 3), from_x(after[4:], 1)
        else:
            far_low, far_high, sent = lax.optimization_barrier((far_low, far_high, sent))
        if l == 4:
            whole = (sent.astype(F32) + pre.astype(F32)).astype(BF16)
            got = lax.ppermute(
                jnp.where(is_layer[4], whole, pre), chips, [(b, a) for a, b in SKIPS]
            )
            carried = jnp.where(is_layer[3], got, carried)
            gskip = jnp.where(early, got, gskip)
        else:
            got = lax.ppermute(sent, chips, between(PLACE[l], PLACE[l - 1]))
            carried = jnp.where(is_layer[l - 1], got, carried)

    rows = grad_low.reshape(2, 8, 16, CELLS)

    rows = lax.all_to_all(rows, "zl", split_axis=1, concat_axis=1)
    rows = lax.all_gather(rows, "core", axis=0, tiled=True)
    rows = lax.all_to_all(rows, "x", split_axis=0, concat_axis=0).reshape(32, 16, CELLS)
    total = pl.pallas_call(
        weight_grad_kernel,
        in_specs=[everywhere] * 6,
        out_shape=pltpu.VMEM((432, 256), BF16),
        compiler_params=limits,
        name="weight_grad",
    )(rows, acts, before, after, far_low, far_high)
    total = lax.all_to_all(
        total.reshape(27, 2, 8, 256), "core", split_axis=1, concat_axis=1
    )
    return total.transpose(2, 0, 1, 3).reshape(1, 8, 27, 512).astype(F32)


def solution(mesh):
    fine = Mesh(mesh.devices.reshape(4, 2, 8, 2, 4), ("y", "zh", "zl", "core", "x"))
    placed = (
        P(None, "x", ("zl", "core")),
        P(("y", "zh"), ("x", "zl", "core"), None, None),
        P(None, "x", ("zl", "core")),
    )
    return jax.shard_map(
        on_device,
        mesh=fine,
        in_specs=placed,
        out_specs=P(("y", "zh"), ("x", "zl", "core"), None, None),
        check_vma=False,
    )
```

```python
import jax
import jax.numpy as jnp
from jax import lax
from jax.experimental import pallas as pl
from jax.experimental.pallas import tpu as pltpu
from jax.sharding import Mesh, PartitionSpec as P

F32 = jnp.float32
BF16 = jnp.bfloat16
LAYERS = 8
CELLS = 128
TAPS = [(df, dh, dw) for df in (-1, 0, 1) for dh in (-1, 0, 1) for dw in (-1, 0, 1)]
PLACE = [0, 1, 3, 5, 4, 2, 6, 7]


def between(source, target):
    crossing = source % 2 != target % 2
    return [(source * 8 + z, target * 8 + (7 - z if crossing else z)) for z in range(8)]


HOMES = [pair for l in range(LAYERS) for pair in between(l, PLACE[l])]
SKIPS = [pair for l in range(LAYERS // 2) for pair in between(PLACE[l], PLACE[7 - l])]
EDGES = (0, 6, 15, 27)
CHUNKS = len(EDGES) - 1
Z_ORDER = [0, 4, 2, 6, 1, 5, 3, 7]
X_ORDER = [0, 2, 1, 3]


def shifted(source, move):
    df, dh, dw = move
    if move == (0, 0, 0):
        return source
    lane = lax.broadcasted_iota(jnp.int32, (1, CELLS), 1)
    f, h, w = lane // 32 + df, (lane // 8) % 4 + dh, lane % 8 + dw
    inside = (f >= 0) & (f < 4) & (h >= 0) & (h < 4) & (w >= 0) & (w < 8)
    turned = pltpu.roll(source, (-(32 * df + 8 * dh + dw)) % CELLS, 1)
    return jnp.where(inside, turned, 0.0)


def tap_rows(kernels, k, blocks=slice(None)):
    chunk = max(c for c in range(CHUNKS) if EDGES[c] <= k)
    return kernels[chunk][blocks, k - EDGES[chunk]].reshape(-1, 256)


def mirror_bits():
    return jnp.where(lax.axis_index("y") == 1, 7, 0)


def carry_out(copies, sems):
    moves = [pltpu.make_async_copy(*copy, sems.at[n]) for n, copy in enumerate(copies)]
    for move in moves:
        move.start()
    for move in moves:
        move.wait()


def place_x_first(gathered, out_ref, sems):
    x, z, flip = lax.axis_index("x"), lax.axis_index("zl"), mirror_bits()
    copies = []
    for q, z_turn in enumerate(Z_ORDER):
        for r, x_turn in enumerate(X_ORDER):
            target = (x ^ x_turn) * 8 + (z ^ z_turn ^ flip)
            copies.append((gathered.at[q * 4 + r], out_ref.at[target]))
    carry_out(copies, sems)


def place_near(own, before, after, out_ref, sems):
    x, z, flip = lax.axis_index("x"), lax.axis_index("zl"), mirror_bits()
    copies = []
    for q, z_turn in enumerate(Z_ORDER):
        for turn, source in ((0, own), (1, after), (3, before)):
            target = ((x + turn) % 4) * 8 + (z ^ z_turn ^ flip)
            copies.append((source.at[q], out_ref.at[target]))
    carry_out(copies, sems)


def place_far(far_low, far_high, held_ref, out_ref, sems):
    x, z, flip = lax.axis_index("x"), lax.axis_index("zl"), mirror_bits()
    copies = []
    for q, z_turn in enumerate(Z_ORDER):
        source = far_low.at[q] if q < 4 else far_high.at[q - 4]
        target = ((x + 2) % 4) * 8 + (z ^ z_turn ^ flip)
        copies.append((source, out_ref.at[target]))
    carry_out(copies, sems)


def forward_kernel(x_ref, skip_ref, *refs):
    kernels, (act_ref, own_ref, other_ref) = refs[:CHUNKS], refs[CHUNKS:]
    core = lax.axis_index("core")
    summed = x_ref[...].astype(F32) + skip_ref[...].astype(F32)
    act = (summed * jax.nn.sigmoid(summed)).astype(BF16)
    act_ref[...] = act
    act = act.astype(F32)
    groups = [range(first, first + 3) for first in range(0, 27, 3)]
    stacks = [
        jnp.concatenate([shifted(act, TAPS[k]).astype(BF16) for k in taps], axis=0)
        for taps in groups
    ]

    def rows(half):
        total = None
        for taps, stacked in zip(groups, stacks):
            matrix = [tap_rows(kernels, k, pl.ds(half * 16, 16)) for k in taps]
            part = lax.dot_general(
                jnp.concatenate(matrix, axis=1),
                stacked,
                (((1,), (0,)), ((), ())),
                preferred_element_type=F32,
            )
            total = part if total is None else total + part
        return total

    other_ref[...] = rows(1 - core).astype(BF16)
    own_ref[...] = rows(core)


def backward_kernel(g_ref, up_ref, gskip_ref, x_ref, skip_ref, *refs):
    kernels, (sent_ref, pre_ref, pad_ref) = refs[:CHUNKS], refs[CHUNKS:]
    grads = g_ref[...].astype(F32).T
    column = lax.broadcasted_iota(jnp.int32, (CELLS, 1), 0) % 8
    pad_ref[...] = jnp.zeros(pad_ref.shape, F32)
    for slot, move in enumerate((1, 0, -1)):
        turned = grads
        if move:
            turned = pltpu.roll(grads, (-move) % CELLS, 0)
            turned = jnp.where((column + move >= 0) & (column + move < 8), turned, 0.0)
        pad_ref[slot, 1:5, 1:5] = turned.reshape(4, 4, 8, 512)
    total = None
    for k, (df, dh, dw) in enumerate(TAPS):
        window = pad_ref[dw + 1, 1 - df : 5 - df, 1 - dh : 5 - dh]
        part = lax.dot_general(
            window.reshape(CELLS, 512).astype(BF16),
            tap_rows(kernels, k),
            (((1,), (0,)), ((), ())),
            preferred_element_type=F32,
        )
        total = part if total is None else total + part
    summed = x_ref[...].astype(F32) + skip_ref[...].astype(F32)
    sig = jax.nn.sigmoid(summed)
    pre = total.T * (sig * (1.0 + summed * (1.0 - sig)))
    pre_ref[...] = pre.astype(BF16)
    upstream = up_ref[...].astype(F32) + gskip_ref[...].astype(F32)
    sent_ref[...] = (upstream + pre).astype(BF16)


def weight_grad_kernel(g_ref, own, before, after, far_low, far_high, out_ref):
    x, z = lax.axis_index("x"), lax.axis_index("zl")
    total = None
    for turn, piece in enumerate((own, after, None, before)):
        for q in range(0, 8, 2):
            left, right = [], []
            for place in (q, q + 1):
                row = ((x + turn) % 4) * 8 + (z ^ Z_ORDER[place])
                grads = g_ref[row].astype(F32)
                left.append(
                    jnp.concatenate(
                        [shifted(grads, tuple(-m for m in move)).astype(BF16) for move in TAPS],
                        axis=0,
                    )
                )
                if piece is not None:
                    right.append(piece[place])
                else:
                    right.append(far_low[place] if place < 4 else far_high[place - 4])
            part = lax.dot_general(
                jnp.concatenate(left, axis=1),
                jnp.concatenate(right, axis=1),
                (((1,), (1,)), ((), ())),
                preferred_element_type=F32,
            )
            total = part if total is None else total + part
    out_ref[...] = total.astype(BF16)


def volume_half(pair, x, section, mirrored):
    picked = [jnp.where(x % 2 == 0, pair[0], pair[1]), jnp.where(x % 2 == 0, pair[1], pair[0])]
    got = []
    for turn in range(2):
        route = []
        for z in range(8):
            for c in range(2):
                for at in range(4):
                    source = ((section * 8 + z) * 2 + c) * 4 + at
                    micro = at % 2 if turn == 0 else 1 - at % 2
                    to = section * 8 + (7 - z if mirrored else z)
                    route.append((source, (to * 2 + at // 2) * 4 + 2 * micro + c))
        got.append(lax.ppermute(picked[turn], ("y", "zh", "zl", "core", "x"), route))
    low = x // 2 == 0
    return jnp.concatenate(
        [jnp.where(low, got[0], got[1]), jnp.where(low, got[1], got[0])], axis=0
    )


def near(*arrays):
    return [pltpu.with_memory_space_constraint(array, pltpu.VMEM) for array in arrays]


def with_z(array, bit):
    other = lax.ppermute(array, "zl", [(i, i ^ bit) for i in range(8)])
    return jnp.concatenate([array, other], axis=0)


def with_x(array, bit):
    other = lax.ppermute(array, "x", [(i, i ^ bit) for i in range(4)])
    return jnp.concatenate([array, other], axis=0)


def from_x(array, distance):
    return lax.ppermute(array, "x", [(i, (i - distance) % 4) for i in range(4)])


def on_device(clips, weights, cotangents):
    y, zh, core, x = (lax.axis_index(a) for a in ("y", "zh", "core", "x"))
    is_layer = [2 * y + zh == PLACE[l] for l in range(LAYERS)]
    early = is_layer[0] | is_layer[1] | is_layer[2]
    first_core = core == 0
    chips = ("y", "zh", "zl")

    x_hold = volume_half(clips, x, PLACE[0], False)
    own = lax.all_to_all(
        weights[0].transpose(1, 0, 2).reshape(27, 8, 2, 256), "core", split_axis=2, concat_axis=1
    ).reshape(27, 16, 256)
    own = lax.ppermute(own, chips, HOMES)
    own, x_hold, is_layer, early, first_core = lax.optimization_barrier(
        (own, x_hold, is_layer, early, first_core)
    )

    everywhere = pl.BlockSpec(memory_space=pltpu.VMEM)
    anywhere = pl.BlockSpec(memory_space=pl.ANY)
    limits = pltpu.CompilerParams(vmem_limit_bytes=20 * 1024 * 1024)

    def place(kernel, *pieces, held=None):
        taps = pieces[0].shape[1]
        operands, specs, aliases = list(pieces), [anywhere] * len(pieces), {}
        if held is not None:
            aliases = {len(operands): 0}
            operands, specs = operands + near(held), specs + [everywhere]
        return pl.pallas_call(
            kernel,
            in_specs=specs,
            out_shape=pltpu.VMEM((32, taps, 16, 256), BF16),
            scratch_shapes=(pltpu.SemaphoreType.DMA((32,)),),
            input_output_aliases=aliases,
            compiler_params=limits,
            name="place_kernels",
        )(*operands)

    parts = [own[None, EDGES[c] : EDGES[c + 1]] for c in range(CHUNKS)]
    parts[0] = with_x(with_x(parts[0], 2), 1)
    for bit in (4, 2, 1):
        for c in range(1, CHUNKS):
            parts[c] = with_z(parts[c], bit)
    kernels = [None]
    for part in parts[1:]:
        before, after = from_x(part, 3), from_x(part, 1)
        far_low, far_high = from_x(before[:4], 3), from_x(after[4:], 1)
        held = place(place_near, part, before, after)
        kernels.append(place(place_far, far_low, far_high, held=held))
    for bit in (4, 2, 1):
        parts[0] = with_z(parts[0], bit)
    kernels[0] = place(place_x_first, parts[0])

    tile = pltpu.VMEM((256, CELLS), BF16)
    forward = pl.pallas_call(
        forward_kernel,
        in_specs=[everywhere] * (2 + CHUNKS),
        out_shape=(tile, pltpu.VMEM((256, CELLS), F32), tile),
        compiler_params=limits,
        name="conv_forward",
    )
    backward = pl.pallas_call(
        backward_kernel,
        out_shape=(tile, tile),
        scratch_shapes=(pltpu.VMEM((3, 6, 6, 8, 512), F32),),
        compiler_params=limits,
        name="conv_backward",
    )

    skip = jnp.zeros((256, CELLS), BF16)
    for l in range(LAYERS):
        act, mine, other = forward(*near(x_hold, skip, *kernels))
        if l == LAYERS - 1:
            break
        both = lax.all_gather(other, "core", axis=0, tiled=False)
        update = mine + jnp.where(first_core, both[1], both[0]).astype(F32)
        out = (x_hold.astype(F32) + update).astype(BF16)
        if l == 0:
            cotangents, out = lax.optimization_barrier((cotangents, out))
            carried = volume_half(cotangents, x, PLACE[7], True)
        elif l == 2:
            carried, out = lax.optimization_barrier((carried, out))
        if l == 3:
            skip = lax.ppermute(out, chips, SKIPS)
            x_hold = jnp.where(is_layer[4], skip, x_hold)
        else:
            got = lax.ppermute(out, chips, between(PLACE[l], PLACE[l + 1]))
            x_hold = jnp.where(is_layer[l + 1], got, x_hold)

    acts = act[None]
    to_home = [(b, a) for a, b in HOMES]
    gskip = jnp.zeros((256, CELLS), BF16)
    for l in reversed(range(LAYERS)):
        grad_low = (carried.astype(F32) + gskip.astype(F32)).astype(BF16)
        if l == 0:
            grad_low = lax.ppermute(grad_low, chips, to_home)
            break
        grads = lax.all_gather(grad_low, "core", axis=0, tiled=True)
        sent, pre = backward(*near(grads, carried, gskip, x_hold, skip, *kernels))
        if l == 7:
            acts, sent = lax.optimization_barrier((acts, sent))
            acts = lax.ppermute(acts, chips, to_home)
        elif l > 3:
            acts, sent = lax.optimization_barrier((acts, sent))
            acts = with_z(acts, 1 << (l - 4))
        elif l == 3:
            acts, sent = lax.optimization_barrier((acts, sent))
            before, after = from_x(acts, 3), from_x(acts, 1)
        elif l == 2:
            before, after, sent = lax.optimization_barrier((before, after, sent))
            far_low, far_high = from_x(before[:4], 3), from_x(after[4:], 1)
        else:
            far_low, far_high, sent = lax.optimization_barrier((far_low, far_high, sent))
        if l == 4:
            whole = (sent.astype(F32) + pre.astype(F32)).astype(BF16)
            got = lax.ppermute(
                jnp.where(is_layer[4], whole, pre), chips, [(b, a) for a, b in SKIPS]
            )
            carried = jnp.where(is_layer[3], got, carried)
            gskip = jnp.where(early, got, gskip)
        else:
            got = lax.ppermute(sent, chips, between(PLACE[l], PLACE[l - 1]))
            carried = jnp.where(is_layer[l - 1], got, carried)

    rows = grad_low.reshape(2, 8, 16, CELLS)

    rows = lax.all_to_all(rows, "zl", split_axis=1, concat_axis=1)
    rows = lax.all_gather(rows, "core", axis=0, tiled=True)
    rows = lax.all_to_all(rows, "x", split_axis=0, concat_axis=0).reshape(32, 16, CELLS)
    total = pl.pallas_call(
        weight_grad_kernel,
        in_specs=[everywhere] * 6,
        out_shape=pltpu.VMEM((432, 256), BF16),
        compiler_params=limits,
        name="weight_grad",
    )(rows, acts, before, after, far_low, far_high)
    total = lax.all_to_all(
        total.reshape(27, 2, 8, 256), "core", split_axis=1, concat_axis=1
    )
    return total.transpose(2, 0, 1, 3).reshape(1, 8, 27, 512).astype(F32)


def solution(mesh):
    fine = Mesh(mesh.devices.reshape(4, 2, 8, 2, 4), ("y", "zh", "zl", "core", "x"))
    placed = (
        P(None, "x", ("zl", "core")),
        P(("y", "zh"), ("x", "zl", "core"), None, None),
        P(None, "x", ("zl", "core")),
    )
    return jax.shard_map(
        on_device,
        mesh=fine,
        in_specs=placed,
        out_specs=P(("y", "zh"), ("x", "zl", "core"), None, None),
        check_vma=False,
    )
```
